32 devices in a mesh: frame: 4 (over y, x), head: 8 (over z, core).
Axes of the slice: x: 2, y: 2, z: 4, core: 2. Of those that a mesh axis runs over, the one named last changes fastest.
Arguments:
- tokens: bfloat16 [4096, 5120], P('frame', 'head'), may hold values from -16 to 16
- qkv_weight: bfloat16 [3, 5120, 2048], P(None, None, 'head'), may hold values from -0.1118034 to 0.1118034
- out_weight: bfloat16 [2048, 5120], P('head'), may hold values from -0.1875 to 0.1875
- modulation: float32 [3, 5120], replicated, may hold values from -3 to 3
- block_mask: int32 [16, 32, 32], P('head', 'frame'), may hold values from 0 to 1, as said below
Outputs:
- mixed: bfloat16 [4096, 5120], P('frame', 'head')
The draws below stay inside these ranges and needn't reach their ends.
Inputs may be any that keep to these rules, and one draw needn't show every extreme that they name: `block_mask`: 1 keeps a pair of 128-token blocks; every query block keeps its own block.
All inputs are finite; a program needn't handle non-finite values.
Results may differ from the reference program's by a relative error of at most 0.0085.
Values may be sent and summed in bfloat16 or wider, within the bound.
A program may use at most 256 MiB of HBM per device.

```python
import math
import jax
import jax.numpy as jnp
from jax import lax

D = 5120
HD = 128
BLK = 128
TPF = 1024
HEADS = 16
N_FRAME = 4


def draw_tokens(key, part):
    first, second = jax.random.split(key, 2)
    seq_len = TPF * N_FRAME
    place = jnp.arange(D, dtype=jnp.float32) / (D - 1)
    rough = jax.random.uniform(second, (D,), jnp.float32, 0.5, 1.5)
    column = 1.0 + 2.0 * place
    values = jax.random.normal(first, (seq_len, D), jnp.float32) * column * rough
    return jnp.clip(values, -16.0, 16.0).astype(jnp.bfloat16)


def draw_qkv_weight(key, part):
    first = jax.random.fold_in(key, 0)
    width = HEADS * HD
    limit = 8.0 / math.sqrt(D)
    values = jax.random.normal(first, (3, D, width), jnp.float32) / math.sqrt(D)
    return jnp.clip(values, -limit, limit).astype(jnp.bfloat16)


def draw_modulation(key, part):
    first, second, third, fourth = jax.random.split(key, 4)
    rough = jax.random.uniform(fourth, (D,), jnp.float32, 0.5, 1.5)
    shift = jnp.clip(0.5 * jax.random.normal(first, (D,), jnp.float32) * rough, -2.5, 2.5)
    scale = jax.random.uniform(second, (D,), jnp.float32, -0.2, 1.0)
    gate = jax.random.uniform(third, (D,), jnp.float32, 0.5, 1.5)
    return jnp.stack([shift, scale, gate])


def draw_block_mask(key, part):
    first, second, third = jax.random.split(key, 3)
    per_frame = TPF // BLK
    frame_count = N_FRAME
    blocks = TPF * N_FRAME // BLK
    spatial = jax.random.randint(first, (HEADS, 1, 1), 0, 2)
    chosen = jax.random.randint(second, (HEADS, frame_count, frame_count), 0, 4) == 0
    extra = jax.random.randint(third, (HEADS, blocks, blocks), 0, 2) == 1
    query_block = jnp.arange(blocks, dtype=jnp.int32)[:, None]
    key_block = jnp.arange(blocks, dtype=jnp.int32)[None, :]
    query_frame = query_block // per_frame
    key_frame = key_block // per_frame
    same = query_frame == key_frame
    pair_chosen = jnp.take_along_axis(chosen.reshape(HEADS, frame_count * frame_count), (query_frame * frame_count + key_frame).reshape(1, -1) * jnp.ones((HEADS, 1), jnp.int32), axis=1).reshape(HEADS, blocks, blocks)
    spatial_keep = same[None] | pair_chosen & extra
    temporal_keep = (key_block % per_frame == query_block % per_frame)[None] | (same & (jnp.abs(query_block - key_block) <= 1))[None]
    keep = jnp.where(spatial == 1, spatial_keep, temporal_keep)
    return keep.astype(jnp.int32)


def spiked(drawn, own_key, source, target, parts, factor):
    owner, partner = [(jnp.arange(drawn.shape[dim]) // (drawn.shape[dim] // parts)).reshape([-1 if axis == dim else 1 for axis in range(drawn.ndim)]) for dim in (source, target)]
    chosen = jax.random.permutation(own_key, parts)[partner]
    strong = (owner == chosen) | (owner == (partner + parts // 2) % parts)
    return jnp.where(strong, factor * drawn, drawn)


def level_of(rng, shape, shards, low, high):
    level, own = 1.0, jax.random.fold_in(rng, 6)
    for dim, shards_of in shards:
        steps = jnp.exp(jax.random.uniform(jax.random.fold_in(own, dim), (shards_of,), jnp.float32, low / len(shards), high / len(shards)))
        level = level * jnp.repeat(steps, shape[dim] // shards_of).reshape([-1 if axis == dim else 1 for axis in range(len(shape))])
    return level


def bell_draw_with(key, extent, scale, reach, pieces, heavy, held_as=jnp.bfloat16):
    values = scale * jax.random.normal(key, extent, jnp.float32)
    if pieces:
        values = values * level_of(key, extent, pieces, -0.22, 0.18)
    return jnp.clip(spiked(values, jax.random.fold_in(key, 3), *heavy), -reach, reach).astype(held_as)


def setup_inputs(seed: int = 0) -> dict:
    splits = jax.random.split(jax.random.key(seed), 6)
    return {
        "tokens": draw_tokens(jax.random.fold_in(splits[5], 71), 0),
        "qkv_weight": draw_qkv_weight(jax.random.fold_in(splits[5], 71), 0),
        "out_weight": bell_draw_with(splits[2], (HEADS * HD, D), (HEADS * HD) ** -0.5, 0.1875, ((0, 8),), (0, 1, 8, 2.0)),
        "modulation": draw_modulation(jax.random.fold_in(splits[5], 71), 0),
        "block_mask": draw_block_mask(jax.random.fold_in(splits[5], 71), 0),
    }


def reference(tokens, qkv_weight, out_weight, modulation, block_mask):
    wide = tokens.astype(jnp.float32)
    center = lax.optimization_barrier(jnp.mean(wide, axis=1, keepdims=True))
    spread = lax.optimization_barrier(jnp.mean(jnp.square(wide - center), axis=1, keepdims=True))
    normed = ((wide - center) * lax.rsqrt(spread + 1e-06) * (1.0 + modulation[1]) + modulation[0]).astype(jnp.bfloat16)
    query = jnp.dot(normed, qkv_weight[0], preferred_element_type=jnp.float32).astype(jnp.bfloat16)
    keyed = jnp.dot(normed, qkv_weight[1], preferred_element_type=jnp.float32).astype(jnp.bfloat16)
    valued = jnp.dot(normed, qkv_weight[2], preferred_element_type=jnp.float32).astype(jnp.bfloat16)
    seq_len = tokens.shape[0]
    heads_count = block_mask.shape[0]
    head_size = qkv_weight.shape[2] // heads_count
    scale = 1.0 / math.sqrt(head_size)

    def split_heads(values):
        return values.reshape(seq_len, heads_count, head_size).transpose(1, 0, 2)

    def one_head(items):
        head_query, head_key, head_value, head_mask = items
        keep = jnp.repeat(jnp.repeat(head_mask > 0, BLK, axis=0), BLK, axis=1)
        scores = jnp.dot(head_query, head_key.T, preferred_element_type=jnp.float32) * scale
        masked = jnp.where(keep, scores, -jnp.inf)
        top = lax.optimization_barrier(jnp.max(masked, axis=1, keepdims=True))
        weights = jnp.where(keep, jnp.exp(scores - top), 0.0)
        total = lax.optimization_barrier(jnp.sum(weights, axis=1, keepdims=True))
        summed = jnp.dot(weights.astype(jnp.bfloat16), head_value, preferred_element_type=jnp.float32)
        return (summed / total).astype(jnp.bfloat16)
    heads_done = lax.map(one_head, (split_heads(query), split_heads(keyed), split_heads(valued), block_mask))
    heads_out = heads_done.transpose(1, 0, 2).reshape(seq_len, heads_count * head_size)
    projected = jnp.dot(heads_out, out_weight, preferred_element_type=jnp.float32)
    return (wide + modulation[2] * projected).astype(jnp.bfloat16)
```

```python
import functools
import math

import jax
import jax.numpy as jnp
from jax import lax
from jax.experimental import pallas as pl
from jax.experimental.pallas import tpu as pltpu
from jax.sharding import PartitionSpec as P

BLK = 128
NEGATIVE = -1e30
EPSILON = 1e-06
LOG2E = math.log2(math.e)
TOKEN_CHUNKS = 4
QUERY_CHUNKS = 2


def partner(size, step):
    if size & (size - 1) == 0:
        return [(i, i ^ step) for i in range(size)]
    return [(i, (i + step) % size) for i in range(size)]


def source_of(me, size, step):
    if size & (size - 1) == 0:
        return lax.bitwise_xor(me, step)
    return lax.rem(me + size - step, size)


def target_of(me, size, step):
    if size & (size - 1) == 0:
        return lax.bitwise_xor(me, step)
    return lax.rem(me + step, size)


def project_kernel(x_ref, shift_ref, gain_ref, w_ref, q_ref, kv_ref, acc_ref, stat_ref):
    step = pl.program_id(0)
    parts, rows, cols = x_ref.shape
    width = parts * cols

    @pl.when(step == 0)
    def _():
        total = jnp.zeros((rows, 1), jnp.float32)
        for i in range(parts):
            total += jnp.sum(x_ref[i].astype(jnp.float32), axis=1, keepdims=True)
        center = total / width
        square = jnp.zeros((rows, 1), jnp.float32)
        for i in range(parts):
            off = x_ref[i].astype(jnp.float32) - center
            square += jnp.sum(off * off, axis=1, keepdims=True)
        stat_ref[0] = jnp.broadcast_to(center, stat_ref.shape[1:])
        stat_ref[1] = jnp.broadcast_to(lax.rsqrt(square / width + EPSILON), stat_ref.shape[1:])
        acc_ref[...] = jnp.zeros_like(acc_ref)

    center = stat_ref[0][:, :1]
    inverse = stat_ref[1][:, :1]
    wide = x_ref[step].astype(jnp.float32)
    normed = ((wide - center) * inverse * (1.0 + gain_ref[0]) + shift_ref[0]).astype(jnp.bfloat16)
    for j in range(3):
        acc_ref[j] += jnp.dot(normed, w_ref[j], preferred_element_type=jnp.float32)

    @pl.when(step == parts - 1)
    def _():
        q_ref[...] = acc_ref[0].astype(q_ref.dtype)
        kv_ref[...] = acc_ref[1:].astype(kv_ref.dtype)


def project(pieces, shift, gain, weight):
    parts, rows, cols = pieces.shape
    inner = weight.shape[2]
    return pl.pallas_call(
        project_kernel,
        grid=(parts,),
        in_specs=[
            pl.BlockSpec((parts, rows, cols), lambda i: (0, 0, 0)),
            pl.BlockSpec((1, 1, cols), lambda i: (i, 0, 0)),
            pl.BlockSpec((1, 1, cols), lambda i: (i, 0, 0)),
            pl.BlockSpec((3, cols, inner), lambda i: (0, i, 0)),
        ],
        out_specs=[
            pl.BlockSpec((rows, inner), lambda i: (0, 0)),
            pl.BlockSpec((2, rows, inner), lambda i: (0, 0, 0)),
        ],
        out_shape=[
            jax.ShapeDtypeStruct((rows, inner), jnp.bfloat16),
            jax.ShapeDtypeStruct((2, rows, inner), jnp.bfloat16),
        ],
        scratch_shapes=[
            pltpu.VMEM((3, rows, inner), jnp.float32),
            pltpu.VMEM((2, rows, 128), jnp.float32),
        ],
        compiler_params=pltpu.CompilerParams(dimension_semantics=("arbitrary",)),
        cost_estimate=pl.CostEstimate(
            flops=6 * parts * cols * rows * inner,
            bytes_accessed=2 * parts * cols * (rows + 3 * inner),
            transcendentals=0,
        ),
        name="project",
    )(pieces, shift, gain, weight)


def attend_kernel(factor, slots, chunks, q_ref, bias_ref, *refs):
    kv_refs, out_ref = refs[:-1], refs[-1]
    rows, head_size = q_ref.shape
    query = q_ref[...]
    top = jnp.full((1, rows), NEGATIVE, jnp.float32)
    total = jnp.zeros((1, rows), jnp.float32)
    summed = jnp.zeros((head_size, rows), jnp.float32)
    for slot in range(slots):
        pieces = []
        block = 0
        new_top = top
        for chunk in range(chunks):
            keys = kv_refs[slot * chunks + chunk][0]
            scores = lax.dot_general(
                keys, query, (((1,), (1,)), ((), ())), preferred_element_type=jnp.float32
            )
            for sub in range(keys.shape[0] // BLK):
                row = bias_ref[0, slot, block : block + 1, :]
                part = scores[sub * BLK : (sub + 1) * BLK] * factor + row
                new_top = jnp.maximum(new_top, jnp.max(part, axis=0, keepdims=True))
                pieces.append(part)
                block += 1
        fade = jnp.exp2(top - new_top)
        total = total * fade
        summed = summed * fade
        per = len(pieces) // chunks
        for chunk in range(chunks):
            values = kv_refs[slot * chunks + chunk][1]
            weights = [jnp.exp2(p - new_top) for p in pieces[chunk * per : (chunk + 1) * per]]
            for w in weights:
                total += jnp.sum(w, axis=0, keepdims=True)
            joined = jnp.concatenate([w.astype(jnp.bfloat16) for w in weights], axis=0)
            summed += lax.dot_general(
                values, joined, (((0,), (0,)), ((), ())), preferred_element_type=jnp.float32
            )
        top = new_top
    out_ref[...] = (summed / total).T.astype(out_ref.dtype)


def attend(query, bias, pieces, slots, heads, tile):
    rows, inner = query.shape
    head_size = inner // heads
    chunks = len(pieces) // slots
    span = pieces[0].shape[1]
    blocks = bias.shape[2]
    factor = LOG2E / math.sqrt(head_size)
    keys_all = span * len(pieces)
    return pl.pallas_call(
        functools.partial(attend_kernel, factor, slots, chunks),
        grid=(heads, rows // tile),
        in_specs=[
            pl.BlockSpec((tile, head_size), lambda h, i: (i, h)),
            pl.BlockSpec((1, slots, blocks, tile), lambda h, i: (h, 0, 0, i)),
        ]
        + [pl.BlockSpec((2, span, head_size), lambda h, i: (0, 0, h))] * len(pieces),
        out_specs=pl.BlockSpec((tile, head_size), lambda h, i: (i, h)),
        out_shape=jax.ShapeDtypeStruct((rows, inner), jnp.bfloat16),
        compiler_params=pltpu.CompilerParams(dimension_semantics=("arbitrary", "arbitrary")),
        cost_estimate=pl.CostEstimate(
            flops=4 * rows * keys_all * inner,
            bytes_accessed=2 * (2 * rows + 2 * keys_all) * inner,
            transcendentals=rows * keys_all * heads,
        ),
        name="attend",
    )(query, bias, *pieces)


def mix_kernel(x_ref, w_ref, tokens_ref, gate_ref, out_ref):
    parts = x_ref.shape[0]
    total = jnp.dot(x_ref[0], w_ref[0], preferred_element_type=jnp.float32)
    for i in range(1, parts):
        total += jnp.dot(x_ref[i], w_ref[i], preferred_element_type=jnp.float32)
    wide = tokens_ref[...].astype(jnp.float32)
    out_ref[...] = (wide + gate_ref[...] * total).astype(out_ref.dtype)


def mix(pieces, weight, tokens, gate, tile):
    parts, rows, inner = pieces.shape
    cols = weight.shape[2]
    return pl.pallas_call(
        mix_kernel,
        grid=(rows // tile,),
        in_specs=[
            pl.BlockSpec((parts, tile, inner), lambda i: (0, i, 0)),
            pl.BlockSpec((parts, inner, cols), lambda i: (0, 0, 0)),
            pl.BlockSpec((tile, cols), lambda i: (i, 0)),
            pl.BlockSpec((1, cols), lambda i: (0, 0)),
        ],
        out_specs=pl.BlockSpec((tile, cols), lambda i: (i, 0)),
        out_shape=jax.ShapeDtypeStruct((rows, cols), jnp.bfloat16),
        compiler_params=pltpu.CompilerParams(dimension_semantics=("arbitrary",)),
        cost_estimate=pl.CostEstimate(
            flops=2 * rows * parts * inner * cols,
            bytes_accessed=2 * parts * inner * (rows + cols) + 4 * rows * cols,
            transcendentals=0,
        ),
        name="mix",
    )(pieces, weight, tokens, gate)


def exchanged_weight(out_weight, frames, heads_axis, local_cols):
    inner = out_weight.shape[0]
    share = inner // frames
    frame, head = lax.axis_index("frame"), lax.axis_index("head")
    mine = lax.dynamic_slice_in_dim(out_weight, frame * share, share, 0)
    arrived = []
    for step in range(heads_axis):
        there = target_of(head, heads_axis, step)
        block = lax.dynamic_slice_in_dim(mine, there * local_cols, local_cols, 1)
        if step:
            block = lax.ppermute(block, "head", partner(heads_axis, step))
        arrived.append(block)
    stacked = jnp.stack(arrived)
    if heads_axis & (heads_axis - 1) == 0:
        order = [lax.bitwise_xor(head, i) for i in range(heads_axis)]
    else:
        order = [lax.rem(head + heads_axis - i, heads_axis) for i in range(heads_axis)]
    ordered = jnp.concatenate([lax.dynamic_slice_in_dim(stacked, i, 1, 0) for i in order])
    shares = [ordered]
    for step in range(1, frames):
        shares.append(lax.ppermute(ordered, "frame", partner(frames, step)))
    stacked = jnp.stack(shares)
    if frames & (frames - 1) == 0:
        order = [lax.bitwise_xor(frame, i) for i in range(frames)]
    else:
        order = [lax.rem(frame + frames - i, frames) for i in range(frames)]
    return jnp.concatenate(
        [lax.dynamic_slice_in_dim(stacked, i, 1, 0)[0] for i in order], axis=1
    )


def shards(frames, heads_axis, tokens, qkv_weight, out_weight, modulation, block_mask):
    local_rows, local_cols = tokens.shape
    heads_here = block_mask.shape[0]
    inner = qkv_weight.shape[2]
    head = lax.axis_index("head")
    frame = lax.axis_index("frame")
    shift = modulation[0].reshape(heads_axis, 1, local_cols)
    gain = modulation[1].reshape(heads_axis, 1, local_cols)
    gate = lax.dynamic_slice_in_dim(modulation[2:3], head * local_cols, local_cols, 1)

    per_frame = local_rows // BLK
    bias = jnp.where(block_mask > 0, 0.0, NEGATIVE).astype(jnp.float32)
    bias = jnp.stack(
        [
            lax.dynamic_slice_in_dim(bias, source_of(frame, frames, s) * per_frame, per_frame, 2)
            for s in range(frames)
        ],
        axis=1,
    )
    bias = jnp.repeat(bias.transpose(0, 1, 3, 2), BLK, axis=3)

    count = TOKEN_CHUNKS
    rows = local_rows // count
    queries, pieces = [], [[None] * count for _ in range(frames)]
    for c in range(count):
        gathered = lax.all_gather(tokens[c * rows : (c + 1) * rows], "head", axis=0)
        query, key_value = project(gathered, shift, gain, qkv_weight)
        queries.append(query)
        pieces[0][c] = key_value
        for s in range(1, frames):
            pieces[s][c] = lax.ppermute(key_value, "frame", partner(frames, s))
    pieces = [p for group in pieces for p in group]

    weight = exchanged_weight(out_weight, frames, heads_axis, local_cols)
    split = QUERY_CHUNKS
    span = local_rows // split
    per = count // split
    outs = []
    for i in range(split):
        query = jnp.concatenate(queries[i * per : (i + 1) * per]) if per > 1 else queries[i]
        part = bias[:, :, :, i * span : (i + 1) * span]
        done = attend(query, part, pieces, frames, heads_here, min(span, 512))
        whole = lax.all_gather(done, "head", axis=0)
        outs.append(mix(whole, weight, tokens[i * span : (i + 1) * span], gate, min(span, 256)))
    return jnp.concatenate(outs)


def solution(mesh):
    placed = (
        P("frame", "head"),
        P(None, None, "head"),
        P("head", None),
        P(),
        P("head", "frame", None),
    )
    body = functools.partial(shards, mesh.shape["frame"], mesh.shape["head"])
    return jax.shard_map(
        body, mesh=mesh, in_specs=placed, out_specs=P("frame", "head"), check_vma=False
    )
```

```python
import functools
import math

import jax
import jax.numpy as jnp
from jax import lax
from jax.experimental import pallas as pl
from jax.experimental.pallas import tpu as pltpu
from jax.sharding import PartitionSpec as P

BLK = 128
NEGATIVE = -1e30
EPSILON = 1e-06
LOG2E = math.log2(math.e)
TOKEN_CHUNKS = 8
QUERY_CHUNKS = 4


def source_of(me, size, step):
    if size & (size - 1) == 0:
        return lax.bitwise_xor(me, step)
    return lax.rem(me + size - step, size)


def target_of(me, size, step):
    if size & (size - 1) == 0:
        return lax.bitwise_xor(me, step)
    return lax.rem(me + step, size)


def chain(me, size):
    return me // 2, me % 2, me + 1 - 2 * (me % 2)


def send(src, dst, send_sem, recv_sem, **where):
    return pltpu.make_async_remote_copy(
        src_ref=src,
        dst_ref=dst,
        send_sem=send_sem,
        recv_sem=recv_sem,
        device_id=where,
        device_id_type=pl.DeviceIdType.MESH,
    )


class Relay:
    def __init__(self, me, size, buffer, span, sems):
        self.me, self.size, self.buffer, self.span = me, size, buffer, span
        self.spot, self.core, self.other = chain(me, size)
        self.line = size // 2
        self.far_send, self.far_recv, self.pair_send, self.pair_recv = sems

    def rows(self, block, chunk):
        start = pl.multiple_of(chunk * self.span, self.span)
        return self.buffer.at[block, pl.ds(start, self.span), :]

    def hop(self, block, chunk, away, source=None):
        ref = self.rows(block, chunk)
        slot = 0 if away > 0 else 1
        return send(
            ref if source is None else source,
            ref,
            self.far_send.at[block // 2, chunk, slot],
            self.far_recv.at[block // 2, chunk],
            head=self.me + 2 * away,
        )

    def pair(self, block, chunk, source=None):
        ref = self.rows(block, chunk)
        return send(
            ref if source is None else source,
            ref,
            self.pair_send.at[block // 2, chunk],
            self.pair_recv.at[block // 2, chunk],
            head=self.other,
        )

    def own(self, chunk, source=None):
        for away in (1, -1):
            edge = self.spot < self.line - 1 if away > 0 else self.spot > 0

            @pl.when(edge)
            def _():
                self.hop(self.me, chunk, away, source).start()

        self.pair(self.me, chunk, source).start()

    def pass_on(self, chunk, distance):
        for away in (1, -1):
            spot = self.spot - away * distance
            here = spot >= 0 if away > 0 else spot < self.line
            edge = self.spot < self.line - 1 if away > 0 else self.spot > 0
            block = spot * 2 + self.core

            @pl.when(here)
            def _():
                self.hop(block, chunk, away).wait_recv()

                @pl.when(edge)
                def _():
                    self.hop(block, chunk, away).start()

                self.pair(block, chunk).start()

    def collect(self, chunk):
        for spot in range(self.line):
            self.pair(spot * 2 + 1 - self.core, chunk).wait_recv()

    def drain(self, chunk):
        for spot in range(self.line):
            block = spot * 2 + self.core
            self.pair(block, chunk).wait_send()
            for away in (1, -1):
                came = spot <= self.spot if away > 0 else spot >= self.spot
                edge = self.spot < self.line - 1 if away > 0 else self.spot > 0

                @pl.when(jnp.logical_and(came, edge))
                def _():
                    self.hop(block, chunk, away).wait_send()


def greet(me, frame, heads_axis, frames):
    barrier = pltpu.get_barrier_semaphore()
    for s in range(1, frames):
        pl.semaphore_signal(
            barrier, inc=1, device_id={"frame": target_of(frame, frames, s)},
            device_id_type=pl.DeviceIdType.MESH,
        )
    for s in range(1, heads_axis):
        pl.semaphore_signal(
            barrier, inc=1, device_id={"head": target_of(me, heads_axis, s)},
            device_id_type=pl.DeviceIdType.MESH,
        )
    pl.semaphore_wait(barrier, frames + heads_axis - 2)


def gather_kernel(
    frames, heads_axis, count, tokens, shift, gain, weight, q_ref, kv_ref,
    got, held, far_send, far_recv, pair_send, pair_recv, kv_send, kv_recv, local,
):
    me, frame = lax.axis_index("head"), lax.axis_index("frame")
    rows, cols = tokens.shape
    span = rows // count
    inner = q_ref.shape[1]
    width = cols * heads_axis
    load = pltpu.make_async_copy(weight, held, local.at[0])
    load.start()
    mine = pltpu.make_async_copy(tokens, got.at[me], local.at[1])
    mine.start()
    greet(me, frame, heads_axis, frames)
    relay = Relay(me, heads_axis, got, span, (far_send, far_recv, pair_send, pair_recv))

    def begin(chunk, carry):
        start = pl.multiple_of(chunk * span, span)
        relay.own(chunk, tokens.at[pl.ds(start, span), :])
        return carry

    lax.fori_loop(0, count, begin, 0)
    mine.wait()
    load.wait()

    def to_frame(chunk, s):
        start = pl.multiple_of(chunk * span, span)
        return send(
            kv_ref.at[0, :, pl.ds(start, span), :],
            kv_ref.at[s, :, pl.ds(start, span), :],
            kv_send.at[chunk, s],
            kv_recv.at[chunk, s],
            frame=target_of(frame, frames, s),
        )

    def step(chunk, carry):
        for distance in range(1, heads_axis // 2):
            relay.pass_on(chunk, distance)
        relay.collect(chunk)
        start = pl.multiple_of(chunk * span, span)
        window = pl.ds(start, span)
        total = jnp.zeros((span, cols), jnp.float32)
        for i in range(heads_axis):
            total += got[i, window, :].astype(jnp.float32)
        center = jnp.sum(total, axis=1, keepdims=True) / width
        square = jnp.zeros((span, cols), jnp.float32)
        for i in range(heads_axis):
            off = got[i, window, :].astype(jnp.float32) - center
            square += off * off
        inverse = lax.rsqrt(jnp.sum(square, axis=1, keepdims=True) / width + EPSILON)
        sums = [jnp.zeros((span, inner), jnp.float32) for _ in range(3)]
        for i in range(heads_axis):
            wide = got[i, window, :].astype(jnp.float32)
            normed = ((wide - center) * inverse * (1.0 + gain[i]) + shift[i]).astype(jnp.bfloat16)
            for j in range(3):
                sums[j] += jnp.dot(
                    normed, held[j, i * cols : (i + 1) * cols, :],
                    preferred_element_type=jnp.float32,
                )
        q_ref[window, :] = sums[0].astype(q_ref.dtype)
        kv_ref[0, 0, window, :] = sums[1].astype(kv_ref.dtype)
        kv_ref[0, 1, window, :] = sums[2].astype(kv_ref.dtype)
        for s in range(1, frames):
            to_frame(chunk, s).start()
        return carry

    lax.fori_loop(0, count, step, 0)

    def finish(chunk, carry):
        relay.drain(chunk)
        for s in range(1, frames):
            to_frame(chunk, s).wait()
        return carry

    lax.fori_loop(0, count, finish, 0)


def gather_project(frames, heads_axis, tokens, shift, gain, weight):
    rows, cols = tokens.shape
    inner = weight.shape[2]
    count = TOKEN_CHUNKS
    line = heads_axis // 2
    whole = pl.BlockSpec(memory_space=pltpu.VMEM)
    away = pl.BlockSpec(memory_space=pl.ANY)
    sem = pltpu.SemaphoreType.DMA
    return pl.pallas_call(
        functools.partial(gather_kernel, frames, heads_axis, count),
        in_specs=[away, whole, whole, away],
        out_specs=[whole, whole],
        out_shape=[
            jax.ShapeDtypeStruct((rows, inner), jnp.bfloat16),
            jax.ShapeDtypeStruct((frames, 2, rows, inner), jnp.bfloat16),
        ],
        scratch_shapes=[
            pltpu.VMEM((heads_axis, rows, cols), jnp.bfloat16),
            pltpu.VMEM(weight.shape, jnp.bfloat16),
            sem((line, count, 2)),
            sem((line, count)),
            sem((line, count)),
            sem((line, count)),
            sem((count, frames)),
            sem((count, frames)),
            sem((2,)),
        ],
        compiler_params=pltpu.CompilerParams(collective_id=0, has_side_effects=True),
        name="gather_project",
    )(tokens, shift, gain, weight)


def attend_kernel(
    frames, heads_axis, heads, count, w_slice, q_ref, kv_ref, bias_ref, weight, tokens, gate,
    out_ref, done, full, far_send, far_recv, pair_send, pair_recv, w_send, w_recv, x_send,
    x_recv, local,
):
    me, frame = lax.axis_index("head"), lax.axis_index("frame")
    rows, inner = q_ref.shape
    head_size = inner // heads
    factor = LOG2E / math.sqrt(head_size)
    span = rows // count
    share = inner // frames
    greet(me, frame, heads_axis, frames)
    relay = Relay(me, heads_axis, done, span, (far_send, far_recv, pair_send, pair_recv))
    band = pl.ds(pl.multiple_of(frame * share, share), share)

    def to_head(s):
        there = target_of(me, heads_axis, s)
        return send(
            w_slice(weight, band, there), full.at[me, band, :], w_send.at[s], w_recv.at[s],
            head=there,
        )

    keep = pltpu.make_async_copy(w_slice(weight, band, me), full.at[me, band, :], local.at[0])
    keep.start()
    for s in range(1, heads_axis):
        to_head(s).start()

    def to_frame(s):
        return send(
            full.at[:, band, :], full.at[:, band, :], x_send.at[s], x_recv.at[s],
            frame=target_of(frame, frames, s),
        )

    def from_frame(s):
        there = source_of(frame, frames, s)
        part = pl.ds(pl.multiple_of(there * share, share), share)
        return send(
            full.at[:, part, :], full.at[:, part, :], x_send.at[s], x_recv.at[s],
            frame=target_of(frame, frames, s),
        )

    def from_head(s):
        there = source_of(me, heads_axis, s)
        ref = full.at[there, band, :]
        return send(ref, ref, w_send.at[s], w_recv.at[s], head=target_of(me, heads_axis, s))

    def tile(t, carry):
        window = pl.ds(pl.multiple_of(t * span, span), span)
        for h in range(heads):
            lanes = slice(h * head_size, (h + 1) * head_size)
            query = q_ref[window, lanes]
            top = jnp.full((1, span), NEGATIVE, jnp.float32)
            total = jnp.zeros((1, span), jnp.float32)
            summed = jnp.zeros((head_size, span), jnp.float32)
            for slot in range(frames):
                scores = lax.dot_general(
                    kv_ref[slot, 0, :, lanes], query, (((1,), (1,)), ((), ())),
                    preferred_element_type=jnp.float32,
                )
                pieces = []
                new_top = top
                for block in range(rows // BLK):
                    row = bias_ref[h, slot, block : block + 1, window]
                    part = scores[block * BLK : (block + 1) * BLK] * factor + row
                    new_top = jnp.maximum(new_top, jnp.max(part, axis=0, keepdims=True))
                    pieces.append(part)
                fade = jnp.exp2(top - new_top)
                total = total * fade
                weights = [jnp.exp2(p - new_top) for p in pieces]
                for w in weights:
                    total += jnp.sum(w, axis=0, keepdims=True)
                joined = jnp.concatenate([w.astype(jnp.bfloat16) for w in weights], axis=0)
                summed = summed * fade + lax.dot_general(
                    kv_ref[slot, 1, :, lanes], joined, (((0,), (0,)), ((), ())),
                    preferred_element_type=jnp.float32,
                )
                top = new_top
            done[me, window, lanes] = (summed / total).T.astype(done.dtype)

        relay.own(t)

        @pl.when(t >= 1)
        def _():
            relay.pass_on(t - 1, 1)

        @pl.when(t == count // 2)
        def _():
            keep.wait()
            for s in range(1, heads_axis):
                from_head(s).wait_recv()
            for s in range(1, frames):
                to_frame(s).start()

        return carry

    lax.fori_loop(0, count, tile, 0)

    def mix(t, carry):
        @pl.when(t == count - 1)
        def _():
            relay.pass_on(t, 1)

        for distance in range(2, heads_axis // 2):
            relay.pass_on(t, distance)
        relay.collect(t)

        @pl.when(t == 0)
        def _():
            for s in range(1, frames):
                from_frame(s).wait_recv()

        window = pl.ds(pl.multiple_of(t * span, span), span)
        total = jnp.zeros(tokens[window, :].shape, jnp.float32)
        for i in range(heads_axis):
            total += jnp.dot(done[i, window, :], full[i], preferred_element_type=jnp.float32)
        wide = tokens[window, :].astype(jnp.float32)
        out_ref[window, :] = (wide + gate[...] * total).astype(out_ref.dtype)
        return carry

    lax.fori_loop(0, count, mix, 0)

    def finish(t, carry):
        relay.drain(t)
        return carry

    lax.fori_loop(0, count, finish, 0)
    for s in range(1, heads_axis):
        to_head(s).wait_send()
    for s in range(1, frames):
        to_frame(s).wait_send()


def attend_mix(frames, heads_axis, heads, query, pairs, bias, out_weight, tokens, gate):
    rows, inner = query.shape
    cols = tokens.shape[1]
    count = QUERY_CHUNKS
    line = heads_axis // 2
    whole = pl.BlockSpec(memory_space=pltpu.VMEM)
    away = pl.BlockSpec(memory_space=pl.ANY)
    sem = pltpu.SemaphoreType.DMA
    if cols % 128 == 0:
        def w_slice(ref, band, there):
            return ref.at[band, pl.ds(pl.multiple_of(there * cols, cols), cols)]
    else:
        out_weight = out_weight.reshape(inner, heads_axis, cols).transpose(1, 0, 2)

        def w_slice(ref, band, there):
            return ref.at[there, band, :]

    return pl.pallas_call(
        functools.partial(attend_kernel, frames, heads_axis, heads, count, w_slice),
        in_specs=[whole, whole, whole, away, whole, whole],
        out_specs=whole,
        out_shape=jax.ShapeDtypeStruct((rows, cols), jnp.bfloat16),
        scratch_shapes=[
            pltpu.VMEM((heads_axis, rows, inner), jnp.bfloat16),
            pltpu.VMEM((heads_axis, inner, cols), jnp.bfloat16),
            sem((line, count, 2)),
            sem((line, count)),
            sem((line, count)),
            sem((line, count)),
            sem((heads_axis,)),
            sem((heads_axis,)),
            sem((frames,)),
            sem((frames,)),
            sem((1,)),
        ],
        compiler_params=pltpu.CompilerParams(collective_id=1, has_side_effects=True),
        name="attend_mix",
    )(query, pairs, bias, out_weight, tokens, gate)


def shards(frames, heads_axis, tokens, qkv_weight, out_weight, modulation, block_mask):
    local_rows, local_cols = tokens.shape
    heads_here = block_mask.shape[0]
    head = lax.axis_index("head")
    frame = lax.axis_index("frame")
    shift = modulation[0].reshape(heads_axis, 1, local_cols)
    gain = modulation[1].reshape(heads_axis, 1, local_cols)
    gate = lax.dynamic_slice_in_dim(modulation[2:3], head * local_cols, local_cols, 1)

    per_frame = local_rows // BLK
    bias = jnp.where(block_mask > 0, 0.0, NEGATIVE).astype(jnp.float32)
    bias = jnp.stack(
        [
            lax.dynamic_slice_in_dim(bias, source_of(frame, frames, s) * per_frame, per_frame, 2)
            for s in range(frames)
        ],
        axis=1,
    )
    bias = jnp.repeat(bias.transpose(0, 1, 3, 2), BLK, axis=3)
    query, pairs = gather_project(frames, heads_axis, tokens, shift, gain, qkv_weight)
    return attend_mix(
        frames, heads_axis, heads_here, query, pairs, bias, out_weight, tokens, gate
    )


def solution(mesh):
    placed = (
        P("frame", "head"),
        P(None, None, "head"),
        P("head", None),
        P(),
        P("head", "frame", None),
    )
    body = functools.partial(shards, mesh.shape["frame"], mesh.shape["head"])
    return jax.shard_map(
        body, mesh=mesh, in_specs=placed, out_specs=P("frame", "head"), check_vma=False
    )
```

```python
import functools
import math

import jax
import jax.numpy as jnp
from jax import lax
from jax.experimental import pallas as pl
from jax.experimental.pallas import tpu as pltpu
from jax.sharding import PartitionSpec as P

BLK = 128
NEGATIVE = -1e30
EPSILON = 1e-06
LOG2E = math.log2(math.e)
TOKEN_CHUNKS = 8
QUERY_CHUNKS = 4


def source_of(me, size, step):
    if size & (size - 1) == 0:
        return lax.bitwise_xor(me, step)
    return lax.rem(me + size - step, size)


def target_of(me, size, step):
    if size & (size - 1) == 0:
        return lax.bitwise_xor(me, step)
    return lax.rem(me + step, size)


def chain(me, size):
    return me // 2, me % 2, me + 1 - 2 * (me % 2)


def send(src, dst, send_sem, recv_sem, **where):
    return pltpu.make_async_remote_copy(
        src_ref=src,
        dst_ref=dst,
        send_sem=send_sem,
        recv_sem=recv_sem,
        device_id=where,
        device_id_type=pl.DeviceIdType.MESH,
    )


class Relay:
    def __init__(self, me, size, buffer, span, sems):
        self.me, self.size, self.buffer, self.span = me, size, buffer, span
        self.spot, self.core, self.other = chain(me, size)
        self.line = size // 2
        self.far_send, self.far_recv, self.pair_send, self.pair_recv = sems

    def rows(self, block, chunk):
        start = pl.multiple_of(chunk * self.span, self.span)
        return self.buffer.at[block, pl.ds(start, self.span), :]

    def hop(self, block, chunk, away, source=None):
        ref = self.rows(block, chunk)
        slot = 0 if away > 0 else 1
        return send(
            ref if source is None else source,
            ref,
            self.far_send.at[block // 2, chunk, slot],
            self.far_recv.at[block // 2, chunk],
            head=self.me + 2 * away,
        )

    def pair(self, block, chunk, source=None):
        ref = self.rows(block, chunk)
        return send(
            ref if source is None else source,
            ref,
            self.pair_send.at[block // 2, chunk],
            self.pair_recv.at[block // 2, chunk],
            head=self.other,
        )

    def own(self, chunk, source=None):
        for away in (1, -1):
            edge = self.spot < self.line - 1 if away > 0 else self.spot > 0

            @pl.when(edge)
            def _():
                self.hop(self.me, chunk, away, source).start()

        self.pair(self.me, chunk, source).start()

    def pass_on(self, chunk, distance):
        for away in (1, -1):
            spot = self.spot - away * distance
            here = spot >= 0 if away > 0 else spot < self.line
            edge = self.spot < self.line - 1 if away > 0 else self.spot > 0
            block = spot * 2 + self.core

            @pl.when(here)
            def _():
                self.hop(block, chunk, away).wait_recv()

                @pl.when(edge)
                def _():
                    self.hop(block, chunk, away).start()

                self.pair(block, chunk).start()

    def advance(self, turn, count):
        for distance in range(1, self.line):
            chunk = turn - (distance - 1)

            @pl.when(jnp.logical_and(chunk >= 0, chunk < count))
            def _():
                self.pass_on(chunk, distance)

    def collect(self, chunk):
        for spot in range(self.line):
            self.pair(spot * 2 + 1 - self.core, chunk).wait_recv()

    def drain(self, chunk):
        for spot in range(self.line):
            block = spot * 2 + self.core
            self.pair(block, chunk).wait_send()
            for away in (1, -1):
                came = spot <= self.spot if away > 0 else spot >= self.spot
                edge = self.spot < self.line - 1 if away > 0 else self.spot > 0

                @pl.when(jnp.logical_and(came, edge))
                def _():
                    self.hop(block, chunk, away).wait_send()


def greet(me, frame, heads_axis, frames):
    barrier = pltpu.get_barrier_semaphore()
    for s in range(1, frames):
        pl.semaphore_signal(
            barrier, inc=1, device_id={"frame": target_of(frame, frames, s)},
            device_id_type=pl.DeviceIdType.MESH,
        )
    for s in range(1, heads_axis):
        pl.semaphore_signal(
            barrier, inc=1, device_id={"head": target_of(me, heads_axis, s)},
            device_id_type=pl.DeviceIdType.MESH,
        )
    pl.semaphore_wait(barrier, frames + heads_axis - 2)


def contract(parts, weight):
    cols = parts[0].shape[1]
    if cols % 128 == 0:
        return jnp.dot(
            jnp.concatenate(parts, axis=1), weight, preferred_element_type=jnp.float32
        )
    total = 0.0
    for i, part in enumerate(parts):
        total += jnp.dot(
            part, weight[i * cols : (i + 1) * cols], preferred_element_type=jnp.float32
        )
    return total


def gather_kernel(
    frames, heads_axis, count, tokens, shift, gain, weight, q_ref, kv_ref,
    got, held, far_send, far_recv, pair_send, pair_recv, kv_send, kv_recv, local,
):
    me, frame = lax.axis_index("head"), lax.axis_index("frame")
    rows, cols = tokens.shape
    span = rows // count
    inner = q_ref.shape[1]
    width = cols * heads_axis
    load = pltpu.make_async_copy(weight, held, local.at[0])
    load.start()
    mine = pltpu.make_async_copy(tokens, got.at[me], local.at[1])
    mine.start()
    greet(me, frame, heads_axis, frames)
    relay = Relay(me, heads_axis, got, span, (far_send, far_recv, pair_send, pair_recv))

    def begin(chunk, carry):
        start = pl.multiple_of(chunk * span, span)
        relay.own(chunk, tokens.at[pl.ds(start, span), :])
        return carry

    lax.fori_loop(0, count, begin, 0)
    mine.wait()
    load.wait()

    def to_frame(chunk, s):
        start = pl.multiple_of(chunk * span, span)
        return send(
            kv_ref.at[0, :, pl.ds(start, span), :],
            kv_ref.at[s, :, pl.ds(start, span), :],
            kv_send.at[chunk, s],
            kv_recv.at[chunk, s],
            frame=target_of(frame, frames, s),
        )

    late = max(heads_axis // 2 - 2, 0)

    def turn(i, carry):
        relay.advance(i, count)

        @pl.when(i >= late)
        def _():
            step(i - late)

        return carry

    def step(chunk):
        relay.collect(chunk)
        start = pl.multiple_of(chunk * span, span)
        window = pl.ds(start, span)
        total = jnp.zeros((span, cols), jnp.float32)
        for i in range(heads_axis):
            total += got[i, window, :].astype(jnp.float32)
        center = jnp.sum(total, axis=1, keepdims=True) / width
        square = jnp.zeros((span, cols), jnp.float32)
        for i in range(heads_axis):
            off = got[i, window, :].astype(jnp.float32) - center
            square += off * off
        inverse = lax.rsqrt(jnp.sum(square, axis=1, keepdims=True) / width + EPSILON)
        parts = []
        for i in range(heads_axis):
            wide = got[i, window, :].astype(jnp.float32)
            parts.append(
                ((wide - center) * inverse * (1.0 + gain[i]) + shift[i]).astype(jnp.bfloat16)
            )
        sums = [contract(parts, held[j]) for j in range(3)]
        q_ref[window, :] = sums[0].astype(q_ref.dtype)
        kv_ref[0, 0, window, :] = sums[1].astype(kv_ref.dtype)
        kv_ref[0, 1, window, :] = sums[2].astype(kv_ref.dtype)
        for s in range(1, frames):
            to_frame(chunk, s).start()

    lax.fori_loop(0, count + late, turn, 0)

    def finish(chunk, carry):
        relay.drain(chunk)
        for s in range(1, frames):
            to_frame(chunk, s).wait()
        return carry

    lax.fori_loop(0, count, finish, 0)


def gather_project(frames, heads_axis, tokens, shift, gain, weight):
    rows, cols = tokens.shape
    inner = weight.shape[2]
    count = TOKEN_CHUNKS
    line = heads_axis // 2
    whole = pl.BlockSpec(memory_space=pltpu.VMEM)
    away = pl.BlockSpec(memory_space=pl.ANY)
    sem = pltpu.SemaphoreType.DMA
    return pl.pallas_call(
        functools.partial(gather_kernel, frames, heads_axis, count),
        in_specs=[away, whole, whole, away],
        out_specs=[whole, whole],
        out_shape=[
            jax.ShapeDtypeStruct((rows, inner), jnp.bfloat16),
            jax.ShapeDtypeStruct((frames, 2, rows, inner), jnp.bfloat16),
        ],
        scratch_shapes=[
            pltpu.VMEM((heads_axis, rows, cols), jnp.bfloat16),
            pltpu.VMEM(weight.shape, jnp.bfloat16),
            sem((line, count, 2)),
            sem((line, count)),
            sem((line, count)),
            sem((line, count)),
            sem((count, frames)),
            sem((count, frames)),
            sem((2,)),
        ],
        compiler_params=pltpu.CompilerParams(collective_id=0, has_side_effects=True),
        name="gather_project",
    )(tokens, shift, gain, weight)


def attend_kernel(
    frames, heads_axis, heads, count, w_slice, q_ref, kv_ref, bias_ref, weight, tokens, gate,
    out_ref, done, full, far_send, far_recv, pair_send, pair_recv, w_send, w_recv, x_send,
    x_recv, local,
):
    me, frame = lax.axis_index("head"), lax.axis_index("frame")
    rows, inner = q_ref.shape
    head_size = inner // heads
    factor = LOG2E / math.sqrt(head_size)
    span = rows // count
    share = inner // frames
    greet(me, frame, heads_axis, frames)
    relay = Relay(me, heads_axis, done, span, (far_send, far_recv, pair_send, pair_recv))
    band = pl.ds(pl.multiple_of(frame * share, share), share)

    def to_head(s):
        there = target_of(me, heads_axis, s)
        return send(
            w_slice(weight, band, there), full.at[me, band, :], w_send.at[s], w_recv.at[s],
            head=there,
        )

    keep = pltpu.make_async_copy(w_slice(weight, band, me), full.at[me, band, :], local.at[0])
    keep.start()
    for s in range(1, heads_axis):
        to_head(s).start()

    def to_frame(s):
        return send(
            full.at[:, band, :], full.at[:, band, :], x_send.at[s], x_recv.at[s],
            frame=target_of(frame, frames, s),
        )

    def from_frame(s):
        there = source_of(frame, frames, s)
        part = pl.ds(pl.multiple_of(there * share, share), share)
        return send(
            full.at[:, part, :], full.at[:, part, :], x_send.at[s], x_recv.at[s],
            frame=target_of(frame, frames, s),
        )

    def from_head(s):
        there = source_of(me, heads_axis, s)
        ref = full.at[there, band, :]
        return send(ref, ref, w_send.at[s], w_recv.at[s], head=target_of(me, heads_axis, s))

    sources = [source_of(frame, frames, s) * (rows // BLK) for s in range(frames)]

    def tile(t, carry):
        window = pl.ds(pl.multiple_of(t * span, span), span)
        for h in range(heads):
            lanes = slice(h * head_size, (h + 1) * head_size)
            query = q_ref[window, lanes]
            top = jnp.full((1, span), NEGATIVE, jnp.float32)
            total = jnp.zeros((1, span), jnp.float32)
            summed = jnp.zeros((head_size, span), jnp.float32)
            for slot in range(frames):
                scores = lax.dot_general(
                    kv_ref[slot, 0, :, lanes], query, (((1,), (1,)), ((), ())),
                    preferred_element_type=jnp.float32,
                )
                pieces = []
                new_top = top
                for block in range(rows // BLK):
                    row = bias_ref[h, pl.ds(sources[slot] + block, 1), window]
                    part = scores[block * BLK : (block + 1) * BLK] * factor + row
                    new_top = jnp.maximum(new_top, jnp.max(part, axis=0, keepdims=True))
                    pieces.append(part)
                fade = jnp.exp2(top - new_top)
                total = total * fade
                weights = [jnp.exp2(p - new_top) for p in pieces]
                for w in weights:
                    total += jnp.sum(w, axis=0, keepdims=True)
                joined = jnp.concatenate([w.astype(jnp.bfloat16) for w in weights], axis=0)
                summed = summed * fade + lax.dot_general(
                    kv_ref[slot, 1, :, lanes], joined, (((0,), (0,)), ((), ())),
                    preferred_element_type=jnp.float32,
                )
                top = new_top
            done[me, window, lanes] = (summed / total).T.astype(done.dtype)

        relay.own(t)

        @pl.when(t >= 1)
        def _():
            relay.advance(t - 1, count)

        @pl.when(t == count // 2)
        def _():
            keep.wait()
            for s in range(1, heads_axis):
                from_head(s).wait_recv()
            for s in range(1, frames):
                to_frame(s).start()

        return carry

    lax.fori_loop(0, count, tile, 0)

    late = max(heads_axis // 2 - 2, 0)

    def rest(i, carry):
        relay.advance(i, count)
        return carry

    lax.fori_loop(count - 1, count + late, rest, 0)
    for s in range(1, frames):
        from_frame(s).wait_recv()

    def out(t, carry):
        relay.collect(t)
        window = pl.ds(pl.multiple_of(t * span, span), span)
        weight = full[...].reshape(heads_axis * inner, full.shape[2])
        total = contract([done[i, window, :] for i in range(heads_axis)], weight)
        wide = tokens[window, :].astype(jnp.float32)
        out_ref[window, :] = (wide + gate[...] * total).astype(out_ref.dtype)
        return carry

    lax.fori_loop(0, count, out, 0)

    def finish(t, carry):
        relay.drain(t)
        return carry

    lax.fori_loop(0, count, finish, 0)
    for s in range(1, heads_axis):
        to_head(s).wait_send()
    for s in range(1, frames):
        to_frame(s).wait_send()


def attend_mix(frames, heads_axis, heads, query, pairs, bias, out_weight, tokens, gate):
    rows, inner = query.shape
    cols = tokens.shape[1]
    count = QUERY_CHUNKS
    line = heads_axis // 2
    whole = pl.BlockSpec(memory_space=pltpu.VMEM)
    away = pl.BlockSpec(memory_space=pl.ANY)
    sem = pltpu.SemaphoreType.DMA
    if cols % 128 == 0:
        def w_slice(ref, band, there):
            return ref.at[band, pl.ds(pl.multiple_of(there * cols, cols), cols)]
    else:
        out_weight = out_weight.reshape(inner, heads_axis, cols).transpose(1, 0, 2)

        def w_slice(ref, band, there):
            return ref.at[there, band, :]

    return pl.pallas_call(
        functools.partial(attend_kernel, frames, heads_axis, heads, count, w_slice),
        in_specs=[whole, whole, whole, away, whole, whole],
        out_specs=whole,
        out_shape=jax.ShapeDtypeStruct((rows, cols), jnp.bfloat16),
        scratch_shapes=[
            pltpu.VMEM((heads_axis, rows, inner), jnp.bfloat16),
            pltpu.VMEM((heads_axis, inner, cols), jnp.bfloat16),
            sem((line, count, 2)),
            sem((line, count)),
            sem((line, count)),
            sem((line, count)),
            sem((heads_axis,)),
            sem((heads_axis,)),
            sem((frames,)),
            sem((frames,)),
            sem((1,)),
        ],
        compiler_params=pltpu.CompilerParams(collective_id=1, has_side_effects=True),
        name="attend_mix",
    )(query, pairs, bias, out_weight, tokens, gate)


def shards(frames, heads_axis, tokens, qkv_weight, out_weight, modulation, block_mask):
    local_rows, local_cols = tokens.shape
    heads_here = block_mask.shape[0]
    head = lax.axis_index("head")
    shift = modulation[0].reshape(heads_axis, 1, local_cols)
    gain = modulation[1].reshape(heads_axis, 1, local_cols)
    gate = lax.dynamic_slice_in_dim(modulation[2:3], head * local_cols, local_cols, 1)

    bias = jnp.where(block_mask > 0, 0.0, NEGATIVE).astype(jnp.float32)
    bias = jnp.repeat(bias.transpose(0, 2, 1), BLK, axis=2)
    query, pairs = gather_project(frames, heads_axis, tokens, shift, gain, qkv_weight)
    return attend_mix(
        frames, heads_axis, heads_here, query, pairs, bias, out_weight, tokens, gate
    )


def solution(mesh):
    placed = (
        P("frame", "head"),
        P(None, None, "head"),
        P("head", None),
        P(),
        P("head", "frame", None),
    )
    body = functools.partial(shards, mesh.shape["frame"], mesh.shape["head"])
    return jax.shard_map(
        body, mesh=mesh, in_specs=placed, out_specs=P("frame", "head"), check_vma=False
    )
```

```python
import functools
import math

import jax
import jax.numpy as jnp
from jax import lax
from jax.experimental import pallas as pl
from jax.experimental.pallas import tpu as pltpu
from jax.sharding import PartitionSpec as P

BLK = 128
NEGATIVE = -1e30
EPSILON = 1e-06
LOG2E = math.log2(math.e)
TOKEN_CHUNKS = 8
QUERY_CHUNKS = 4


def source_of(me, size, step):
    if size & (size - 1) == 0:
        return lax.bitwise_xor(me, step)
    return lax.rem(me + size - step, size)


def target_of(me, size, step):
    if size & (size - 1) == 0:
        return lax.bitwise_xor(me, step)
    return lax.rem(me + step, size)


def chain(me, size):
    return me // 2, me % 2, me + 1 - 2 * (me % 2)


def send(src, dst, send_sem, recv_sem, **where):
    return pltpu.make_async_remote_copy(
        src_ref=src,
        dst_ref=dst,
        send_sem=send_sem,
        recv_sem=recv_sem,
        device_id=where,
        device_id_type=pl.DeviceIdType.MESH,
    )


class Relay:
    def __init__(self, me, size, buffer, span, sems):
        self.me, self.size, self.buffer, self.span = me, size, buffer, span
        self.spot, self.core, self.other = chain(me, size)
        self.line = size // 2
        self.far_send, self.far_recv, self.pair_send, self.pair_recv = sems

    def rows(self, block, chunk):
        start = pl.multiple_of(chunk * self.span, self.span)
        return self.buffer.at[block, pl.ds(start, self.span), :]

    def hop(self, block, chunk, away, source=None):
        ref = self.rows(block, chunk)
        slot = 0 if away > 0 else 1
        return send(
            ref if source is None else source,
            ref,
            self.far_send.at[block // 2, chunk, slot],
            self.far_recv.at[block // 2, chunk],
            head=self.me + 2 * away,
        )

    def pair(self, block, chunk, source=None):
        ref = self.rows(block, chunk)
        return send(
            ref if source is None else source,
            ref,
            self.pair_send.at[block // 2, chunk],
            self.pair_recv.at[block // 2, chunk],
            head=self.other,
        )

    def own(self, chunk, source=None):
        for away in (1, -1):
            edge = self.spot < self.line - 1 if away > 0 else self.spot > 0

            @pl.when(edge)
            def _():
                self.hop(self.me, chunk, away, source).start()

        self.pair(self.me, chunk, source).start()

    def pass_on(self, chunk, distance):
        for away in (1, -1):
            spot = self.spot - away * distance
            here = spot >= 0 if away > 0 else spot < self.line
            edge = self.spot < self.line - 1 if away > 0 else self.spot > 0
            block = spot * 2 + self.core

            @pl.when(here)
            def _():
                self.hop(block, chunk, away).wait_recv()

                @pl.when(edge)
                def _():
                    self.hop(block, chunk, away).start()

                self.pair(block, chunk).start()

    def advance(self, turn, count):
        for distance in range(1, self.line):
            chunk = turn - (distance - 1)

            @pl.when(jnp.logical_and(chunk >= 0, chunk < count))
            def _():
                self.pass_on(chunk, distance)

    def collect(self, chunk):
        for spot in range(self.line):
            self.pair(spot * 2 + 1 - self.core, chunk).wait_recv()

    def drain(self, chunk):
        for spot in range(self.line):
            block = spot * 2 + self.core
            self.pair(block, chunk).wait_send()
            for away in (1, -1):
                came = spot <= self.spot if away > 0 else spot >= self.spot
                edge = self.spot < self.line - 1 if away > 0 else self.spot > 0

                @pl.when(jnp.logical_and(came, edge))
                def _():
                    self.hop(block, chunk, away).wait_send()


def greet(me, frame, heads_axis, frames):
    barrier = pltpu.get_barrier_semaphore()
    for s in range(1, frames):
        pl.semaphore_signal(
            barrier, inc=1, device_id={"frame": target_of(frame, frames, s)},
            device_id_type=pl.DeviceIdType.MESH,
        )
    for s in range(1, heads_axis):
        pl.semaphore_signal(
            barrier, inc=1, device_id={"head": target_of(me, heads_axis, s)},
            device_id_type=pl.DeviceIdType.MESH,
        )
    pl.semaphore_wait(barrier, frames + heads_axis - 2)


def contract(parts, weight):
    cols = parts[0].shape[1]
    if cols % 128 == 0:
        return jnp.dot(
            jnp.concatenate(parts, axis=1), weight, preferred_element_type=jnp.float32
        )
    total = 0.0
    for i, part in enumerate(parts):
        total += jnp.dot(
            part, weight[i * cols : (i + 1) * cols], preferred_element_type=jnp.float32
        )
    return total


def gather_kernel(
    frames, heads_axis, count, w_slice, tokens, modulation, weight, out_weight, q_ref, kv_ref,
    band_ref, got, held, far_send, far_recv, pair_send, pair_recv, kv_send, kv_recv, w_send,
    w_recv, local,
):
    me, frame = lax.axis_index("head"), lax.axis_index("frame")
    rows, cols = tokens.shape
    span = rows // count
    inner = q_ref.shape[1]
    width = cols * heads_axis
    load = pltpu.make_async_copy(weight, held, local.at[0])
    load.start()
    mine = pltpu.make_async_copy(tokens, got.at[me], local.at[1])
    mine.start()
    share = band_ref.shape[1]
    band = pl.ds(pl.multiple_of(frame * share, share), share)
    keep = pltpu.make_async_copy(w_slice(out_weight, band, me), band_ref.at[me], local.at[2])
    keep.start()
    greet(me, frame, heads_axis, frames)
    relay = Relay(me, heads_axis, got, span, (far_send, far_recv, pair_send, pair_recv))

    def begin(chunk, carry):
        start = pl.multiple_of(chunk * span, span)
        relay.own(chunk, tokens.at[pl.ds(start, span), :])
        return carry

    lax.fori_loop(0, count, begin, 0)
    mine.wait()
    load.wait()

    def to_frame(chunk, s):
        start = pl.multiple_of(chunk * span, span)
        return send(
            kv_ref.at[0, :, pl.ds(start, span), :],
            kv_ref.at[s, :, pl.ds(start, span), :],
            kv_send.at[chunk, s],
            kv_recv.at[chunk, s],
            frame=target_of(frame, frames, s),
        )

    def to_head(s):
        there = target_of(me, heads_axis, s)
        return send(
            w_slice(out_weight, band, there), band_ref.at[me], w_send.at[s], w_recv.at[s],
            head=there,
        )

    late = max(heads_axis // 2 - 2, 0)

    def turn(i, carry):
        relay.advance(i, count)

        @pl.when(i == count + late - 2)
        def _():
            for s in range(1, heads_axis):
                to_head(s).start()

        @pl.when(i >= late)
        def _():
            step(i - late)

        return carry

    def step(chunk):
        relay.collect(chunk)
        start = pl.multiple_of(chunk * span, span)
        window = pl.ds(start, span)
        total = jnp.zeros((span, cols), jnp.float32)
        for i in range(heads_axis):
            total += got[i, window, :].astype(jnp.float32)
        center = jnp.sum(total, axis=1, keepdims=True) / width
        square = jnp.zeros((span, cols), jnp.float32)
        for i in range(heads_axis):
            off = got[i, window, :].astype(jnp.float32) - center
            square += off * off
        inverse = lax.rsqrt(jnp.sum(square, axis=1, keepdims=True) / width + EPSILON)
        parts = []
        for i in range(heads_axis):
            wide = got[i, window, :].astype(jnp.float32)
            shift = modulation[0:1, i * cols : (i + 1) * cols]
            gain = modulation[1:2, i * cols : (i + 1) * cols]
            parts.append(
                ((wide - center) * inverse * (1.0 + gain) + shift).astype(jnp.bfloat16)
            )
        sums = [contract(parts, held[j]) for j in range(3)]
        q_ref[window, :] = sums[0].astype(q_ref.dtype)
        kv_ref[0, 0, window, :] = sums[1].astype(kv_ref.dtype)
        kv_ref[0, 1, window, :] = sums[2].astype(kv_ref.dtype)
        for s in range(1, frames):
            to_frame(chunk, s).start()

    lax.fori_loop(0, count + late, turn, 0)

    def finish(chunk, carry):
        relay.drain(chunk)
        for s in range(1, frames):
            to_frame(chunk, s).wait()
        return carry

    lax.fori_loop(0, count, finish, 0)
    keep.wait()
    for s in range(1, heads_axis):
        there = source_of(me, heads_axis, s)
        ref = band_ref.at[there]
        send(ref, ref, w_send.at[s], w_recv.at[s], head=target_of(me, heads_axis, s)).wait_recv()
        to_head(s).wait_send()


def gather_project(frames, heads_axis, tokens, modulation, weight, out_weight):
    rows, cols = tokens.shape
    inner = weight.shape[2]
    count = TOKEN_CHUNKS
    line = heads_axis // 2
    whole = pl.BlockSpec(memory_space=pltpu.VMEM)
    away = pl.BlockSpec(memory_space=pl.ANY)
    sem = pltpu.SemaphoreType.DMA
    if cols % 128 == 0:
        def w_slice(ref, band, there):
            return ref.at[band, pl.ds(pl.multiple_of(there * cols, cols), cols)]
    else:
        out_weight = out_weight.reshape(inner, heads_axis, cols).transpose(1, 0, 2)

        def w_slice(ref, band, there):
            return ref.at[there, band, :]

    return pl.pallas_call(
        functools.partial(gather_kernel, frames, heads_axis, count, w_slice),
        in_specs=[away, whole, away, away],
        out_specs=[whole, whole, whole],
        out_shape=[
            jax.ShapeDtypeStruct((rows, inner), jnp.bfloat16),
            jax.ShapeDtypeStruct((frames, 2, rows, inner), jnp.bfloat16),
            jax.ShapeDtypeStruct((heads_axis, inner // frames, cols), jnp.bfloat16),
        ],
        scratch_shapes=[
            pltpu.VMEM((heads_axis, rows, cols), jnp.bfloat16),
            pltpu.VMEM(weight.shape, jnp.bfloat16),
            sem((line, count, 2)),
            sem((line, count)),
            sem((line, count)),
            sem((line, count)),
            sem((count, frames)),
            sem((count, frames)),
            sem((heads_axis,)),
            sem((heads_axis,)),
            sem((3,)),
        ],
        compiler_params=pltpu.CompilerParams(collective_id=0, has_side_effects=True),
        name="gather_project",
    )(tokens, modulation, weight, out_weight)


def attend_kernel(
    frames, heads_axis, heads, count, q_ref, kv_ref, bias_ref, band_ref, tokens, gate,
    out_ref, done, full, far_send, far_recv, pair_send, pair_recv, x_send, x_recv, local,
):
    me, frame = lax.axis_index("head"), lax.axis_index("frame")
    rows, inner = q_ref.shape
    head_size = inner // heads
    factor = LOG2E / math.sqrt(head_size)
    span = rows // count
    share = inner // frames
    greet(me, frame, heads_axis, frames)
    relay = Relay(me, heads_axis, done, span, (far_send, far_recv, pair_send, pair_recv))
    band = pl.ds(pl.multiple_of(frame * share, share), share)

    keep = pltpu.make_async_copy(band_ref, full.at[:, band, :], local.at[0])
    keep.start()

    def to_frame(s):
        return send(
            band_ref, full.at[:, band, :], x_send.at[s], x_recv.at[s],
            frame=target_of(frame, frames, s),
        )

    def from_frame(s):
        there = source_of(frame, frames, s)
        part = pl.ds(pl.multiple_of(there * share, share), share)
        return send(
            full.at[:, part, :], full.at[:, part, :], x_send.at[s], x_recv.at[s],
            frame=target_of(frame, frames, s),
        )

    for s in range(1, frames):
        to_frame(s).start()
    sources = [source_of(frame, frames, s) * (rows // BLK) for s in range(frames)]

    def tile(t, carry):
        window = pl.ds(pl.multiple_of(t * span, span), span)
        for h in range(heads):
            lanes = slice(h * head_size, (h + 1) * head_size)
            query = q_ref[window, lanes]
            top = jnp.full((1, span), NEGATIVE, jnp.float32)
            total = jnp.zeros((1, span), jnp.float32)
            summed = jnp.zeros((head_size, span), jnp.float32)
            for slot in range(frames):
                scores = lax.dot_general(
                    kv_ref[slot, 0, :, lanes], query, (((1,), (1,)), ((), ())),
                    preferred_element_type=jnp.float32,
                )
                pieces = []
                new_top = top
                for block in range(rows // BLK):
                    row = bias_ref[h, pl.ds(sources[slot] + block, 1), window]
                    part = scores[block * BLK : (block + 1) * BLK] * factor + row
                    new_top = jnp.maximum(new_top, jnp.max(part, axis=0, keepdims=True))
                    pieces.append(part)
                fade = jnp.exp2(top - new_top)
                total = total * fade
                weights = [jnp.exp2(p - new_top) for p in pieces]
                for w in weights:
                    total += jnp.sum(w, axis=0, keepdims=True)
                joined = jnp.concatenate([w.astype(jnp.bfloat16) for w in weights], axis=0)
                summed = summed * fade + lax.dot_general(
                    kv_ref[slot, 1, :, lanes], joined, (((0,), (0,)), ((), ())),
                    preferred_element_type=jnp.float32,
                )
                top = new_top
            done[me, window, lanes] = (summed / total).T.astype(done.dtype)

        relay.own(t)

        @pl.when(t >= 1)
        def _():
            relay.advance(t - 1, count)

        return carry

    lax.fori_loop(0, count, tile, 0)

    late = max(heads_axis // 2 - 2, 0)

    def rest(i, carry):
        relay.advance(i, count)
        return carry

    lax.fori_loop(count - 1, count + late - 1, rest, 0)
    keep.wait()
    for s in range(1, frames):
        from_frame(s).wait_recv()

    def out(t, carry):
        @pl.when(t == count - 1)
        def _():
            relay.advance(count + late - 1, count)

        relay.collect(t)
        window = pl.ds(pl.multiple_of(t * span, span), span)
        weight = full[...].reshape(heads_axis * inner, full.shape[2])
        total = contract([done[i, window, :] for i in range(heads_axis)], weight)
        wide = tokens[window, :].astype(jnp.float32)
        out_ref[window, :] = (wide + gate[...] * total).astype(out_ref.dtype)
        return carry

    lax.fori_loop(0, count, out, 0)

    def finish(t, carry):
        relay.drain(t)
        return carry

    lax.fori_loop(0, count, finish, 0)
    for s in range(1, frames):
        to_frame(s).wait_send()


def attend_mix(frames, heads_axis, heads, query, pairs, bias, band, tokens, gate):
    rows, inner = query.shape
    cols = tokens.shape[1]
    count = QUERY_CHUNKS
    line = heads_axis // 2
    whole = pl.BlockSpec(memory_space=pltpu.VMEM)
    away = pl.BlockSpec(memory_space=pl.ANY)
    sem = pltpu.SemaphoreType.DMA
    return pl.pallas_call(
        functools.partial(attend_kernel, frames, heads_axis, heads, count),
        in_specs=[whole] * 6,
        out_specs=whole,
        out_shape=jax.ShapeDtypeStruct((rows, cols), jnp.bfloat16),
        scratch_shapes=[
            pltpu.VMEM((heads_axis, rows, inner), jnp.bfloat16),
            pltpu.VMEM((heads_axis, inner, cols), jnp.bfloat16),
            sem((line, count, 2)),
            sem((line, count)),
            sem((line, count)),
            sem((line, count)),
            sem((frames,)),
            sem((frames,)),
            sem((1,)),
        ],
        compiler_params=pltpu.CompilerParams(collective_id=1, has_side_effects=True),
        name="attend_mix",
    )(query, pairs, bias, band, tokens, gate)


def shards(frames, heads_axis, tokens, qkv_weight, out_weight, modulation, block_mask):
    local_rows, local_cols = tokens.shape
    heads_here = block_mask.shape[0]
    head = lax.axis_index("head")
    gate = lax.dynamic_slice_in_dim(modulation[2:3], head * local_cols, local_cols, 1)

    bias = jnp.where(block_mask > 0, 0.0, NEGATIVE).astype(jnp.float32)
    bias = jnp.repeat(bias.transpose(0, 2, 1), BLK, axis=2)
    query, pairs, band = gather_project(
        frames, heads_axis, tokens, modulation, qkv_weight, out_weight
    )
    return attend_mix(frames, heads_axis, heads_here, query, pairs, bias, band, tokens, gate)


def solution(mesh):
    placed = (
        P("frame", "head"),
        P(None, None, "head"),
        P("head", None),
        P(),
        P("head", "frame", None),
    )
    body = functools.partial(shards, mesh.shape["frame"], mesh.shape["head"])
    return jax.shard_map(
        body, mesh=mesh, in_specs=placed, out_specs=P("frame", "head"), check_vma=False
    )
```

```python
import functools
import math

import jax
import jax.numpy as jnp
from jax import lax
from jax.experimental import pallas as pl
from jax.experimental.pallas import tpu as pltpu
from jax.sharding import PartitionSpec as P

BLK = 128
NEGATIVE = -1e30
EPSILON = 1e-06
LOG2E = math.log2(math.e)
TOKEN_CHUNKS = 8
QUERY_CHUNKS = 4


def source_of(me, size, step):
    if size & (size - 1) == 0:
        return lax.bitwise_xor(me, step)
    return lax.rem(me + size - step, size)


def target_of(me, size, step):
    if size & (size - 1) == 0:
        return lax.bitwise_xor(me, step)
    return lax.rem(me + step, size)


def chain(me, size):
    return me // 2, me % 2, me + 1 - 2 * (me % 2)


def send(src, dst, send_sem, recv_sem, **where):
    return pltpu.make_async_remote_copy(
        src_ref=src,
        dst_ref=dst,
        send_sem=send_sem,
        recv_sem=recv_sem,
        device_id=where,
        device_id_type=pl.DeviceIdType.MESH,
    )


class Relay:
    def __init__(self, me, size, buffer, span, sems):
        self.me, self.size, self.buffer, self.span = me, size, buffer, span
        self.spot, self.core, self.other = chain(me, size)
        self.line = size // 2
        self.far_send, self.far_recv, self.pair_send, self.pair_recv = sems

    def rows(self, block, chunk):
        start = pl.multiple_of(chunk * self.span, self.span)
        return self.buffer.at[block, pl.ds(start, self.span), :]

    def hop(self, block, chunk, away, source=None):
        ref = self.rows(block, chunk)
        slot = 0 if away > 0 else 1
        return send(
            ref if source is None else source,
            ref,
            self.far_send.at[block // 2, chunk, slot],
            self.far_recv.at[block // 2, chunk],
            head=self.me + 2 * away,
        )

    def pair(self, block, chunk, source=None):
        ref = self.rows(block, chunk)
        return send(
            ref if source is None else source,
            ref,
            self.pair_send.at[block // 2, chunk],
            self.pair_recv.at[block // 2, chunk],
            head=self.other,
        )

    def own(self, chunk, source=None):
        for away in (1, -1):
            edge = self.spot < self.line - 1 if away > 0 else self.spot > 0

            @pl.when(edge)
            def _():
                self.hop(self.me, chunk, away, source).start()

        self.pair(self.me, chunk, source).start()

    def pass_on(self, chunk, distance):
        for away in (1, -1):
            spot = self.spot - away * distance
            here = spot >= 0 if away > 0 else spot < self.line
            edge = self.spot < self.line - 1 if away > 0 else self.spot > 0
            block = spot * 2 + self.core

            @pl.when(here)
            def _():
                self.hop(block, chunk, away).wait_recv()

                @pl.when(edge)
                def _():
                    self.hop(block, chunk, away).start()

                self.pair(block, chunk).start()

    def advance(self, turn, count):
        for distance in range(1, self.line):
            chunk = turn - (distance - 1)

            @pl.when(jnp.logical_and(chunk >= 0, chunk < count))
            def _():
                self.pass_on(chunk, distance)

    def collect(self, chunk):
        for spot in range(self.line):
            self.pair(spot * 2 + 1 - self.core, chunk).wait_recv()

    def drain(self, chunk):
        for spot in range(self.line):
            block = spot * 2 + self.core
            self.pair(block, chunk).wait_send()
            for away in (1, -1):
                came = spot <= self.spot if away > 0 else spot >= self.spot
                edge = self.spot < self.line - 1 if away > 0 else self.spot > 0

                @pl.when(jnp.logical_and(came, edge))
                def _():
                    self.hop(block, chunk, away).wait_send()


def greet(me, frame, heads_axis, frames):
    barrier = pltpu.get_barrier_semaphore()
    for s in range(1, frames):
        pl.semaphore_signal(
            barrier, inc=1, device_id={"frame": target_of(frame, frames, s)},
            device_id_type=pl.DeviceIdType.MESH,
        )
    for s in range(1, heads_axis):
        pl.semaphore_signal(
            barrier, inc=1, device_id={"head": target_of(me, heads_axis, s)},
            device_id_type=pl.DeviceIdType.MESH,
        )
    pl.semaphore_wait(barrier, frames + heads_axis - 2)


def contract(parts, weight):
    cols = parts[0].shape[1]
    if cols % 128 == 0:
        return jnp.dot(
            jnp.concatenate(parts, axis=1), weight, preferred_element_type=jnp.float32
        )
    total = 0.0
    for i, part in enumerate(parts):
        total += jnp.dot(
            part, weight[i * cols : (i + 1) * cols], preferred_element_type=jnp.float32
        )
    return total


def gather_kernel(
    frames, heads_axis, count, w_slice, tokens, modulation, weight, out_weight, q_ref, kv_ref,
    band_ref, got, held, far_send, far_recv, pair_send, pair_recv, kv_send, kv_recv, w_send,
    w_recv, local,
):
    me, frame = lax.axis_index("head"), lax.axis_index("frame")
    rows, cols = tokens.shape
    span = rows // count
    inner = q_ref.shape[1]
    width = cols * heads_axis
    load = pltpu.make_async_copy(weight, held, local.at[0])
    load.start()
    mine = pltpu.make_async_copy(tokens, got.at[me], local.at[1])
    mine.start()
    share = band_ref.shape[1]
    band = pl.ds(pl.multiple_of(frame * share, share), share)
    keep = pltpu.make_async_copy(w_slice(out_weight, band, me), band_ref.at[me], local.at[2])
    keep.start()
    greet(me, frame, heads_axis, frames)
    relay = Relay(me, heads_axis, got, span, (far_send, far_recv, pair_send, pair_recv))

    def begin(chunk, carry):
        start = pl.multiple_of(chunk * span, span)
        relay.own(chunk, tokens.at[pl.ds(start, span), :])
        return carry

    lax.fori_loop(0, count, begin, 0)
    mine.wait()
    load.wait()

    def to_frame(chunk, s):
        start = pl.multiple_of(chunk * span, span)
        return send(
            kv_ref.at[0, :, pl.ds(start, span), :],
            kv_ref.at[s, :, pl.ds(start, span), :],
            kv_send.at[chunk, s],
            kv_recv.at[chunk, s],
            frame=target_of(frame, frames, s),
        )

    def to_head(s):
        there = target_of(me, heads_axis, s)
        return send(
            w_slice(out_weight, band, there), band_ref.at[me], w_send.at[s], w_recv.at[s],
            head=there,
        )

    late = max(heads_axis // 2 - 2, 0)

    def turn(i, carry):
        relay.advance(i, count)

        @pl.when(i == count + late - 2)
        def _():
            for s in range(1, heads_axis):
                to_head(s).start()

        @pl.when(i >= late)
        def _():
            step(i - late)

        return carry

    def step(chunk):
        relay.collect(chunk)
        start = pl.multiple_of(chunk * span, span)
        window = pl.ds(start, span)
        total = jnp.zeros((span, cols), jnp.float32)
        for i in range(heads_axis):
            total += got[i, window, :].astype(jnp.float32)
        center = jnp.sum(total, axis=1, keepdims=True) / width
        square = jnp.zeros((span, cols), jnp.float32)
        for i in range(heads_axis):
            off = got[i, window, :].astype(jnp.float32) - center
            square += off * off
        inverse = lax.rsqrt(jnp.sum(square, axis=1, keepdims=True) / width + EPSILON)
        parts = []
        for i in range(heads_axis):
            wide = got[i, window, :].astype(jnp.float32)
            shift = modulation[0:1, i * cols : (i + 1) * cols]
            gain = modulation[1:2, i * cols : (i + 1) * cols]
            parts.append(
                ((wide - center) * inverse * (1.0 + gain) + shift).astype(jnp.bfloat16)
            )
        sums = [contract(parts, held[j]) for j in range(3)]
        q_ref[window, :] = sums[0].astype(q_ref.dtype)
        kv_ref[0, 0, window, :] = sums[1].astype(kv_ref.dtype)
        kv_ref[0, 1, window, :] = sums[2].astype(kv_ref.dtype)
        for s in range(1, frames):
            to_frame(chunk, s).start()

    lax.fori_loop(0, count + late, turn, 0)

    def finish(chunk, carry):
        relay.drain(chunk)
        for s in range(1, frames):
            to_frame(chunk, s).wait()
        return carry

    lax.fori_loop(0, count, finish, 0)
    keep.wait()
    for s in range(1, heads_axis):
        there = source_of(me, heads_axis, s)
        ref = band_ref.at[there]
        send(ref, ref, w_send.at[s], w_recv.at[s], head=target_of(me, heads_axis, s)).wait_recv()
        to_head(s).wait_send()


def gather_project(frames, heads_axis, tokens, modulation, weight, out_weight):
    rows, cols = tokens.shape
    inner = weight.shape[2]
    count = TOKEN_CHUNKS
    line = heads_axis // 2
    whole = pl.BlockSpec(memory_space=pltpu.VMEM)
    away = pl.BlockSpec(memory_space=pl.ANY)
    sem = pltpu.SemaphoreType.DMA
    if cols % 128 == 0:
        def w_slice(ref, band, there):
            return ref.at[band, pl.ds(pl.multiple_of(there * cols, cols), cols)]
    else:
        out_weight = out_weight.reshape(inner, heads_axis, cols).transpose(1, 0, 2)

        def w_slice(ref, band, there):
            return ref.at[there, band, :]

    return pl.pallas_call(
        functools.partial(gather_kernel, frames, heads_axis, count, w_slice),
        in_specs=[away, whole, away, away],
        out_specs=[whole, whole, whole],
        out_shape=[
            jax.ShapeDtypeStruct((rows, inner), jnp.bfloat16),
            jax.ShapeDtypeStruct((frames, 2, rows, inner), jnp.bfloat16),
            jax.ShapeDtypeStruct((heads_axis, inner // frames, cols), jnp.bfloat16),
        ],
        scratch_shapes=[
            pltpu.VMEM((heads_axis, rows, cols), jnp.bfloat16),
            pltpu.VMEM(weight.shape, jnp.bfloat16),
            sem((line, count, 2)),
            sem((line, count)),
            sem((line, count)),
            sem((line, count)),
            sem((count, frames)),
            sem((count, frames)),
            sem((heads_axis,)),
            sem((heads_axis,)),
            sem((3,)),
        ],
        compiler_params=pltpu.CompilerParams(collective_id=0, has_side_effects=True),
        name="gather_project",
    )(tokens, modulation, weight, out_weight)


def attend_kernel(
    frames, heads_axis, heads, count, q_ref, kv_ref, mask_ref, band_ref, tokens, gate,
    out_ref, done, full, far_send, far_recv, pair_send, pair_recv, x_send, x_recv, local,
):
    me, frame = lax.axis_index("head"), lax.axis_index("frame")
    rows, inner = q_ref.shape
    head_size = inner // heads
    factor = LOG2E / math.sqrt(head_size)
    span = rows // count
    share = inner // frames
    greet(me, frame, heads_axis, frames)
    relay = Relay(me, heads_axis, done, span, (far_send, far_recv, pair_send, pair_recv))
    band = pl.ds(pl.multiple_of(frame * share, share), share)

    keep = pltpu.make_async_copy(band_ref, full.at[:, band, :], local.at[0])
    keep.start()

    def to_frame(s):
        return send(
            band_ref, full.at[:, band, :], x_send.at[s], x_recv.at[s],
            frame=target_of(frame, frames, s),
        )

    def from_frame(s):
        there = source_of(frame, frames, s)
        part = pl.ds(pl.multiple_of(there * share, share), share)
        return send(
            full.at[:, part, :], full.at[:, part, :], x_send.at[s], x_recv.at[s],
            frame=target_of(frame, frames, s),
        )

    for s in range(1, frames):
        to_frame(s).start()
    sources = [source_of(frame, frames, s) * (rows // BLK) for s in range(frames)]

    wide = span // BLK

    def tile(t, carry):
        window = pl.ds(pl.multiple_of(t * span, span), span)
        for h in range(heads):
            lanes = slice(h * head_size, (h + 1) * head_size)
            query = q_ref[window, lanes]
            top = jnp.full((1, span), NEGATIVE, jnp.float32)
            total = jnp.zeros((1, span), jnp.float32)
            summed = jnp.zeros((head_size, span), jnp.float32)
            for slot in range(frames):
                scores = lax.dot_general(
                    kv_ref[slot, 0, :, lanes], query, (((1,), (1,)), ((), ())),
                    preferred_element_type=jnp.float32,
                )
                pieces = []
                new_top = top
                for block in range(rows // BLK):
                    row = jnp.concatenate(
                        [
                            jnp.full(
                                (1, BLK),
                                jnp.where(
                                    mask_ref[h, t * wide + k, sources[slot] + block] > 0,
                                    0.0,
                                    NEGATIVE,
                                ),
                                jnp.float32,
                            )
                            for k in range(wide)
                        ],
                        axis=1,
                    )
                    part = scores[block * BLK : (block + 1) * BLK] * factor + row
                    new_top = jnp.maximum(new_top, jnp.max(part, axis=0, keepdims=True))
                    pieces.append(part)
                fade = jnp.exp2(top - new_top)
                total = total * fade
                weights = [jnp.exp2(p - new_top) for p in pieces]
                for w in weights:
                    total += jnp.sum(w, axis=0, keepdims=True)
                joined = jnp.concatenate([w.astype(jnp.bfloat16) for w in weights], axis=0)
                summed = summed * fade + lax.dot_general(
                    kv_ref[slot, 1, :, lanes], joined, (((0,), (0,)), ((), ())),
                    preferred_element_type=jnp.float32,
                )
                top = new_top
            done[me, window, lanes] = (summed / total).T.astype(done.dtype)

        relay.own(t)

        @pl.when(t >= 1)
        def _():
            relay.advance(t - 1, count)

        return carry

    lax.fori_loop(0, count, tile, 0)

    late = max(heads_axis // 2 - 2, 0)

    def rest(i, carry):
        relay.advance(i, count)
        return carry

    lax.fori_loop(count - 1, count + late - 1, rest, 0)
    keep.wait()
    for s in range(1, frames):
        from_frame(s).wait_recv()

    def out(t, carry):
        @pl.when(t == count - 1)
        def _():
            relay.advance(count + late - 1, count)

        relay.collect(t)
        window = pl.ds(pl.multiple_of(t * span, span), span)
        weight = full[...].reshape(heads_axis * inner, full.shape[2])
        total = contract([done[i, window, :] for i in range(heads_axis)], weight)
        if gate.shape[1] == out_ref.shape[1]:
            own = gate[...]
        else:
            cols = out_ref.shape[1]
            own = gate[2:3, pl.ds(pl.multiple_of(me * cols, cols), cols)]
        held = tokens[window, :].astype(jnp.float32)
        out_ref[window, :] = (held + own * total).astype(out_ref.dtype)
        return carry

    lax.fori_loop(0, count, out, 0)

    def finish(t, carry):
        relay.drain(t)
        return carry

    lax.fori_loop(0, count, finish, 0)
    for s in range(1, frames):
        to_frame(s).wait_send()


def attend_mix(frames, heads_axis, heads, query, pairs, mask, band, tokens, gate):
    rows, inner = query.shape
    cols = tokens.shape[1]
    count = QUERY_CHUNKS
    line = heads_axis // 2
    whole = pl.BlockSpec(memory_space=pltpu.VMEM)
    away = pl.BlockSpec(memory_space=pl.ANY)
    sem = pltpu.SemaphoreType.DMA
    return pl.pallas_call(
        functools.partial(attend_kernel, frames, heads_axis, heads, count),
        in_specs=[whole, whole, pl.BlockSpec(memory_space=pltpu.SMEM), whole, whole, whole],
        out_specs=whole,
        out_shape=jax.ShapeDtypeStruct((rows, cols), jnp.bfloat16),
        scratch_shapes=[
            pltpu.VMEM((heads_axis, rows, inner), jnp.bfloat16),
            pltpu.VMEM((heads_axis, inner, cols), jnp.bfloat16),
            sem((line, count, 2)),
            sem((line, count)),
            sem((line, count)),
            sem((line, count)),
            sem((frames,)),
            sem((frames,)),
            sem((1,)),
        ],
        compiler_params=pltpu.CompilerParams(collective_id=1, has_side_effects=True),
        name="attend_mix",
    )(query, pairs, mask, band, tokens, gate)


def shards(frames, heads_axis, tokens, qkv_weight, out_weight, modulation, block_mask):
    local_rows, local_cols = tokens.shape
    heads_here = block_mask.shape[0]
    head = lax.axis_index("head")
    gate = modulation
    if local_cols % 128:
        gate = lax.dynamic_slice_in_dim(modulation[2:3], head * local_cols, local_cols, 1)

    query, pairs, band = gather_project(
        frames, heads_axis, tokens, modulation, qkv_weight, out_weight
    )
    return attend_mix(frames, heads_axis, heads_here, query, pairs, block_mask, band, tokens, gate)


def solution(mesh):
    placed = (
        P("frame", "head"),
        P(None, None, "head"),
        P("head", None),
        P(),
        P("head", "frame", None),
    )
    body = functools.partial(shards, mesh.shape["frame"], mesh.shape["head"])
    return jax.shard_map(
        body, mesh=mesh, in_specs=placed, out_specs=P("frame", "head"), check_vma=False
    )
```

```python
import functools
import math

import jax
import jax.numpy as jnp
from jax import lax
from jax.experimental import pallas as pl
from jax.experimental.pallas import tpu as pltpu
from jax.sharding import PartitionSpec as P

BLK = 128
NEGATIVE = -1e30
EPSILON = 1e-06
LOG2E = math.log2(math.e)
TOKEN_CHUNKS = 8
QUERY_CHUNKS = 8


def source_of(me, size, step):
    if size & (size - 1) == 0:
        return lax.bitwise_xor(me, step)
    return lax.rem(me + size - step, size)


def target_of(me, size, step):
    if size & (size - 1) == 0:
        return lax.bitwise_xor(me, step)
    return lax.rem(me + step, size)


def chain(me, size):
    return me // 2, me % 2, me + 1 - 2 * (me % 2)


def send(src, dst, send_sem, recv_sem, **where):
    return pltpu.make_async_remote_copy(
        src_ref=src,
        dst_ref=dst,
        send_sem=send_sem,
        recv_sem=recv_sem,
        device_id=where,
        device_id_type=pl.DeviceIdType.MESH,
    )


class Relay:
    def __init__(self, me, size, buffer, span, sems):
        self.me, self.size, self.buffer, self.span = me, size, buffer, span
        self.spot, self.core, self.other = chain(me, size)
        self.line = size // 2
        self.far_send, self.far_recv, self.pair_send, self.pair_recv = sems

    def rows(self, block, chunk):
        start = pl.multiple_of(chunk * self.span, self.span)
        return self.buffer.at[block, pl.ds(start, self.span), :]

    def hop(self, block, chunk, away, source=None):
        ref = self.rows(block, chunk)
        slot = 0 if away > 0 else 1
        return send(
            ref if source is None else source,
            ref,
            self.far_send.at[block // 2, chunk, slot],
            self.far_recv.at[block // 2, chunk],
            head=self.me + 2 * away,
        )

    def pair(self, block, chunk, source=None):
        ref = self.rows(block, chunk)
        return send(
            ref if source is None else source,
            ref,
            self.pair_send.at[block // 2, chunk],
            self.pair_recv.at[block // 2, chunk],
            head=self.other,
        )

    def own(self, chunk, source=None):
        for away in (1, -1):
            edge = self.spot < self.line - 1 if away > 0 else self.spot > 0

            @pl.when(edge)
            def _():
                self.hop(self.me, chunk, away, source).start()

        self.pair(self.me, chunk, source).start()

    def pass_on(self, chunk, distance):
        for away in (1, -1):
            spot = self.spot - away * distance
            here = spot >= 0 if away > 0 else spot < self.line
            edge = self.spot < self.line - 1 if away > 0 else self.spot > 0
            block = spot * 2 + self.core

            @pl.when(here)
            def _():
                self.hop(block, chunk, away).wait_recv()

                @pl.when(edge)
                def _():
                    self.hop(block, chunk, away).start()

                self.pair(block, chunk).start()

    def advance(self, turn, count):
        for distance in range(1, self.line):
            chunk = turn - (distance - 1)

            @pl.when(jnp.logical_and(chunk >= 0, chunk < count))
            def _():
                self.pass_on(chunk, distance)

    def collect(self, chunk):
        for spot in range(self.line):
            self.pair(spot * 2 + 1 - self.core, chunk).wait_recv()

    def drain(self, chunk):
        for spot in range(self.line):
            block = spot * 2 + self.core
            self.pair(block, chunk).wait_send()
            for away in (1, -1):
                came = spot <= self.spot if away > 0 else spot >= self.spot
                edge = self.spot < self.line - 1 if away > 0 else self.spot > 0

                @pl.when(jnp.logical_and(came, edge))
                def _():
                    self.hop(block, chunk, away).wait_send()


def greet(me, frame, heads_axis, frames):
    barrier = pltpu.get_barrier_semaphore()
    for s in range(1, frames):
        pl.semaphore_signal(
            barrier, inc=1, device_id={"frame": target_of(frame, frames, s)},
            device_id_type=pl.DeviceIdType.MESH,
        )
    for s in range(1, heads_axis):
        pl.semaphore_signal(
            barrier, inc=1, device_id={"head": target_of(me, heads_axis, s)},
            device_id_type=pl.DeviceIdType.MESH,
        )
    pl.semaphore_wait(barrier, frames + heads_axis - 2)


def contract(parts, weight):
    cols = parts[0].shape[1]
    if cols % 128 == 0:
        return jnp.dot(
            jnp.concatenate(parts, axis=1), weight, preferred_element_type=jnp.float32
        )
    total = 0.0
    for i, part in enumerate(parts):
        total += jnp.dot(
            part, weight[i * cols : (i + 1) * cols], preferred_element_type=jnp.float32
        )
    return total


def gather_kernel(
    frames, heads_axis, count, w_slice, tokens, modulation, weight, out_weight, q_ref, kv_ref,
    band_ref, got, held, far_send, far_recv, pair_send, pair_recv, kv_send, kv_recv, w_send,
    w_recv, local,
):
    me, frame = lax.axis_index("head"), lax.axis_index("frame")
    rows, cols = tokens.shape
    span = rows // count
    inner = q_ref.shape[1]
    width = cols * heads_axis
    load = pltpu.make_async_copy(weight, held, local.at[0])
    load.start()
    mine = pltpu.make_async_copy(tokens, got.at[me], local.at[1])
    mine.start()
    share = band_ref.shape[1]
    band = pl.ds(pl.multiple_of(frame * share, share), share)
    keep = pltpu.make_async_copy(w_slice(out_weight, band, me), band_ref.at[me], local.at[2])
    keep.start()
    greet(me, frame, heads_axis, frames)
    relay = Relay(me, heads_axis, got, span, (far_send, far_recv, pair_send, pair_recv))

    def begin(chunk, carry):
        start = pl.multiple_of(chunk * span, span)
        relay.own(chunk, tokens.at[pl.ds(start, span), :])
        return carry

    lax.fori_loop(0, count, begin, 0)
    mine.wait()
    load.wait()

    def to_frame(chunk, s):
        start = pl.multiple_of(chunk * span, span)
        return send(
            kv_ref.at[0, :, pl.ds(start, span), :],
            kv_ref.at[s, :, pl.ds(start, span), :],
            kv_send.at[chunk, s],
            kv_recv.at[chunk, s],
            frame=target_of(frame, frames, s),
        )

    def to_head(s):
        there = target_of(me, heads_axis, s)
        return send(
            w_slice(out_weight, band, there), band_ref.at[me], w_send.at[s], w_recv.at[s],
            head=there,
        )

    late = max(heads_axis // 2 - 2, 0)

    def turn(i, carry):
        relay.advance(i, count)

        @pl.when(i == count + late - 2)
        def _():
            for s in range(1, heads_axis):
                to_head(s).start()

        @pl.when(i >= late)
        def _():
            step(i - late)

        return carry

    def step(chunk):
        relay.collect(chunk)
        start = pl.multiple_of(chunk * span, span)
        window = pl.ds(start, span)
        total = jnp.zeros((span, cols), jnp.float32)
        for i in range(heads_axis):
            total += got[i, window, :].astype(jnp.float32)
        center = jnp.sum(total, axis=1, keepdims=True) / width
        square = jnp.zeros((span, cols), jnp.float32)
        for i in range(heads_axis):
            off = got[i, window, :].astype(jnp.float32) - center
            square += off * off
        inverse = lax.rsqrt(jnp.sum(square, axis=1, keepdims=True) / width + EPSILON)
        parts = []
        for i in range(heads_axis):
            wide = got[i, window, :].astype(jnp.float32)
            shift = modulation[0:1, i * cols : (i + 1) * cols]
            gain = modulation[1:2, i * cols : (i + 1) * cols]
            parts.append(
                ((wide - center) * inverse * (1.0 + gain) + shift).astype(jnp.bfloat16)
            )
        sums = [contract(parts, held[j]) for j in range(3)]
        q_ref[window, :] = sums[0].astype(q_ref.dtype)
        kv_ref[0, 0, window, :] = sums[1].astype(kv_ref.dtype)
        kv_ref[0, 1, window, :] = sums[2].astype(kv_ref.dtype)
        for s in range(1, frames):
            to_frame(chunk, s).start()

    lax.fori_loop(0, count + late, turn, 0)

    def finish(chunk, carry):
        relay.drain(chunk)
        for s in range(1, frames):
            to_frame(chunk, s).wait()
        return carry

    lax.fori_loop(0, count, finish, 0)
    keep.wait()
    for s in range(1, heads_axis):
        there = source_of(me, heads_axis, s)
        ref = band_ref.at[there]
        send(ref, ref, w_send.at[s], w_recv.at[s], head=target_of(me, heads_axis, s)).wait_recv()
        to_head(s).wait_send()


def gather_project(frames, heads_axis, tokens, modulation, weight, out_weight):
    rows, cols = tokens.shape
    inner = weight.shape[2]
    count = TOKEN_CHUNKS
    line = heads_axis // 2
    whole = pl.BlockSpec(memory_space=pltpu.VMEM)
    away = pl.BlockSpec(memory_space=pl.ANY)
    sem = pltpu.SemaphoreType.DMA
    if cols % 128 == 0:
        def w_slice(ref, band, there):
            return ref.at[band, pl.ds(pl.multiple_of(there * cols, cols), cols)]
    else:
        out_weight = out_weight.reshape(inner, heads_axis, cols).transpose(1, 0, 2)

        def w_slice(ref, band, there):
            return ref.at[there, band, :]

    return pl.pallas_call(
        functools.partial(gather_kernel, frames, heads_axis, count, w_slice),
        in_specs=[away, whole, away, away],
        out_specs=[whole, whole, whole],
        out_shape=[
            jax.ShapeDtypeStruct((rows, inner), jnp.bfloat16),
            jax.ShapeDtypeStruct((frames, 2, rows, inner), jnp.bfloat16),
            jax.ShapeDtypeStruct((heads_axis, inner // frames, cols), jnp.bfloat16),
        ],
        scratch_shapes=[
            pltpu.VMEM((heads_axis, rows, cols), jnp.bfloat16),
            pltpu.VMEM(weight.shape, jnp.bfloat16),
            sem((line, count, 2)),
            sem((line, count)),
            sem((line, count)),
            sem((line, count)),
            sem((count, frames)),
            sem((count, frames)),
            sem((heads_axis,)),
            sem((heads_axis,)),
            sem((3,)),
        ],
        compiler_params=pltpu.CompilerParams(collective_id=0, has_side_effects=True),
        name="gather_project",
    )(tokens, modulation, weight, out_weight)


def attend_kernel(
    frames, heads_axis, heads, count, q_ref, kv_ref, mask_ref, band_ref, tokens, gate,
    out_ref, done, full, far_send, far_recv, pair_send, pair_recv, x_send, x_recv, local,
):
    me, frame = lax.axis_index("head"), lax.axis_index("frame")
    rows, inner = q_ref.shape
    head_size = inner // heads
    factor = LOG2E / math.sqrt(head_size)
    span = rows // count
    share = inner // frames
    greet(me, frame, heads_axis, frames)
    relay = Relay(me, heads_axis, done, span, (far_send, far_recv, pair_send, pair_recv))
    band = pl.ds(pl.multiple_of(frame * share, share), share)

    keep = pltpu.make_async_copy(band_ref, full.at[:, band, :], local.at[0])
    keep.start()

    def to_frame(s):
        return send(
            band_ref, full.at[:, band, :], x_send.at[s], x_recv.at[s],
            frame=target_of(frame, frames, s),
        )

    def from_frame(s):
        there = source_of(frame, frames, s)
        part = pl.ds(pl.multiple_of(there * share, share), share)
        return send(
            full.at[:, part, :], full.at[:, part, :], x_send.at[s], x_recv.at[s],
            frame=target_of(frame, frames, s),
        )

    for s in range(1, frames):
        to_frame(s).start()
    sources = [source_of(frame, frames, s) * (rows // BLK) for s in range(frames)]

    wide = span // BLK

    def tile(t, carry):
        window = pl.ds(pl.multiple_of(t * span, span), span)
        for h in range(heads):
            lanes = slice(h * head_size, (h + 1) * head_size)
            query = q_ref[window, lanes]
            top = jnp.full((1, span), NEGATIVE, jnp.float32)
            total = jnp.zeros((1, span), jnp.float32)
            summed = jnp.zeros((head_size, span), jnp.float32)
            for slot in range(frames):
                scores = lax.dot_general(
                    kv_ref[slot, 0, :, lanes], query, (((1,), (1,)), ((), ())),
                    preferred_element_type=jnp.float32,
                )
                pieces = []
                new_top = top
                for block in range(rows // BLK):
                    row = jnp.concatenate(
                        [
                            jnp.full(
                                (1, BLK),
                                jnp.where(
                                    mask_ref[h, t * wide + k, sources[slot] + block] > 0,
                                    0.0,
                                    NEGATIVE,
                                ),
                                jnp.float32,
                            )
                            for k in range(wide)
                        ],
                        axis=1,
                    )
                    part = scores[block * BLK : (block + 1) * BLK] * factor + row
                    new_top = jnp.maximum(new_top, jnp.max(part, axis=0, keepdims=True))
                    pieces.append(part)
                fade = jnp.exp2(top - new_top)
                total = total * fade
                weights = [jnp.exp2(p - new_top) for p in pieces]
                for w in weights:
                    total += jnp.sum(w, axis=0, keepdims=True)
                joined = jnp.concatenate([w.astype(jnp.bfloat16) for w in weights], axis=0)
                summed = summed * fade + lax.dot_general(
                    kv_ref[slot, 1, :, lanes], joined, (((0,), (0,)), ((), ())),
                    preferred_element_type=jnp.float32,
                )
                top = new_top
            done[me, window, lanes] = (summed / total).T.astype(done.dtype)

        relay.own(t)

        @pl.when(t >= 1)
        def _():
            relay.advance(t - 1, count)

        return carry

    lax.fori_loop(0, count, tile, 0)

    late = max(heads_axis // 2 - 2, 0)

    def rest(i, carry):
        relay.advance(i, count)
        return carry

    lax.fori_loop(count - 1, count + late - 1, rest, 0)
    keep.wait()
    for s in range(1, frames):
        from_frame(s).wait_recv()

    def out(t, carry):
        @pl.when(t == count - 1)
        def _():
            relay.advance(count + late - 1, count)

        relay.collect(t)
        window = pl.ds(pl.multiple_of(t * span, span), span)
        weight = full[...].reshape(heads_axis * inner, full.shape[2])
        total = contract([done[i, window, :] for i in range(heads_axis)], weight)
        if gate.shape[1] == out_ref.shape[1]:
            own = gate[...]
        else:
            cols = out_ref.shape[1]
            own = gate[2:3, pl.ds(pl.multiple_of(me * cols, cols), cols)]
        held = tokens[window, :].astype(jnp.float32)
        out_ref[window, :] = (held + own * total).astype(out_ref.dtype)
        return carry

    lax.fori_loop(0, count, out, 0)

    def finish(t, carry):
        relay.drain(t)
        return carry

    lax.fori_loop(0, count, finish, 0)
    for s in range(1, frames):
        to_frame(s).wait_send()


def attend_mix(frames, heads_axis, heads, query, pairs, mask, band, tokens, gate):
    rows, inner = query.shape
    cols = tokens.shape[1]
    count = QUERY_CHUNKS
    line = heads_axis // 2
    whole = pl.BlockSpec(memory_space=pltpu.VMEM)
    away = pl.BlockSpec(memory_space=pl.ANY)
    sem = pltpu.SemaphoreType.DMA
    return pl.pallas_call(
        functools.partial(attend_kernel, frames, heads_axis, heads, count),
        in_specs=[whole, whole, pl.BlockSpec(memory_space=pltpu.SMEM), whole, whole, whole],
        out_specs=whole,
        out_shape=jax.ShapeDtypeStruct((rows, cols), jnp.bfloat16),
        scratch_shapes=[
            pltpu.VMEM((heads_axis, rows, inner), jnp.bfloat16),
            pltpu.VMEM((heads_axis, inner, cols), jnp.bfloat16),
            sem((line, count, 2)),
            sem((line, count)),
            sem((line, count)),
            sem((line, count)),
            sem((frames,)),
            sem((frames,)),
            sem((1,)),
        ],
        compiler_params=pltpu.CompilerParams(collective_id=1, has_side_effects=True),
        name="attend_mix",
    )(query, pairs, mask, band, tokens, gate)


def shards(frames, heads_axis, tokens, qkv_weight, out_weight, modulation, block_mask):
    local_rows, local_cols = tokens.shape
    heads_here = block_mask.shape[0]
    head = lax.axis_index("head")
    gate = modulation
    if local_cols % 128:
        gate = lax.dynamic_slice_in_dim(modulation[2:3], head * local_cols, local_cols, 1)

    query, pairs, band = gather_project(
        frames, heads_axis, tokens, modulation, qkv_weight, out_weight
    )
    return attend_mix(frames, heads_axis, heads_here, query, pairs, block_mask, band, tokens, gate)


def solution(mesh):
    placed = (
        P("frame", "head"),
        P(None, None, "head"),
        P("head", None),
        P(),
        P("head", "frame", None),
    )
    body = functools.partial(shards, mesh.shape["frame"], mesh.shape["head"])
    return jax.shard_map(
        body, mesh=mesh, in_specs=placed, out_specs=P("frame", "head"), check_vma=False
    )
```
